32 devices in a mesh: ctx: 8 (over z, y), head: 4 (over x, core).
Axes of the slice: x: 2, y: 2, z: 4, core: 2. Of those that a mesh axis runs over, the one named last changes fastest.
Arguments:
- query_act: bfloat16 [2048, 2048], P('ctx', 'head'), may hold values from -5 to 5
- key_act: bfloat16 [2048, 2048], P('ctx', 'head'), may hold values from -5 to 5
- value_act: bfloat16 [2048, 2048], P('ctx', 'head'), may hold values from -6 to 6
- out_weight: bfloat16 [2048, 2048], P('head'), may hold values from -0.125 to 0.125
- cotangent: bfloat16 [2048, 2048], P('ctx', 'head'), may hold values from -6 to 6
- butterfly_cols: int32 [16, 3], replicated, may hold values from 0 to 15, as said below
- global_cols: int32 [256], replicated, may hold values from 0 to 2047, as said below
Outputs:
- layer_out: bfloat16 [2048, 2048], P('ctx', 'head')
- query_grad: bfloat16 [2048, 2048], P('ctx', 'head')
- key_grad: bfloat16 [2048, 2048], P('ctx', 'head')
- value_grad: bfloat16 [2048, 2048], P('ctx', 'head')
The draws below stay inside these ranges and needn't reach their ends.
Inputs may be any that keep to these rules, and one draw needn't show every extreme that they name: `butterfly_cols`: entry [i, l] names one of the 2 blocks with index in the group (i // 2) xor 2**l, groups being runs of 2 consecutive block indices. `global_cols`: the positions are distinct.
All inputs are finite; a program needn't handle non-finite values.
Results may differ from the reference program's by a relative error of at most 0.0068.
Values may be sent and summed in bfloat16 or wider, within the bound.
No kernel may reach another device: no remote copies, remote signals or barrier semaphores. Data moves between devices by JAX's collectives and lax.ppermute only.
A program may use at most 64 MiB of HBM per device.

```python
import jax
import jax.numpy as jnp
from jax import lax

HEADS = 16
HEAD_SIZE = 128
BLOCK = 128
LEVELS = 3
GLOBALS = 256
D = 2048
TOKENS = 2048
NBLK = 16
BLK_DEV = 2


def drawn_pair(key):
    first = jax.random.fold_in(key, 11)
    second = jax.random.fold_in(key, 12)
    queries = jnp.clip(jax.random.normal(first, (TOKENS, D), jnp.float32), -4.5, 4.5)
    keyset = jnp.clip(jax.random.normal(second, (TOKENS, D), jnp.float32), -4.5, 4.5)
    return (queries, keyset)


def draw_query_act(key, part):
    return drawn_pair(key)[0].astype(jnp.bfloat16)


def draw_key_act(key, part):
    return drawn_pair(key)[1].astype(jnp.bfloat16)


def draw_butterfly_cols(key, part):
    rows = jnp.arange(NBLK, dtype=jnp.int32)
    home = rows // BLK_DEV
    strides = jnp.arange(LEVELS, dtype=jnp.int32)
    partner = jnp.bitwise_xor(home[:, None], jnp.left_shift(jnp.int32(1), strides)[None, :])
    inner = jax.random.randint(jax.random.fold_in(key, 5), (NBLK, LEVELS), 0, BLK_DEV, dtype=jnp.int32)
    first_stride = strides[None, :] == 0
    inner = jnp.where(jnp.logical_and(first_stride, home[:, None] == NBLK // BLK_DEV - 2), BLK_DEV - 1, inner)
    inner = jnp.where(jnp.logical_and(first_stride, home[:, None] == 1), 0, inner)
    return (partner * BLK_DEV + inner).astype(jnp.int32)


def draw_global_cols(key, part):
    inner = 1 + jax.random.permutation(jax.random.fold_in(key, 7), TOKENS - 2)[:GLOBALS - 2]
    chosen = jnp.concatenate([jnp.array([0, TOKENS - 1], jnp.int32), inner.astype(jnp.int32)])
    shuffle = jax.random.permutation(jax.random.fold_in(key, 9), GLOBALS)
    return chosen[shuffle].astype(jnp.int32)


def steps_of(key, shape, pieces, smallest, high):
    def one(axis_at, parts):
        heights = jax.random.uniform(jax.random.fold_in(jax.random.fold_in(key, 6), axis_at), (parts,), jnp.float32, smallest / len(pieces), high / len(pieces))
        return jnp.repeat(jnp.exp(heights), shape[axis_at] // parts).reshape((-1,) + (1,) * (len(shape) - axis_at - 1))

    factor_of = one(*pieces[0])
    for cut in pieces[1:]:
        factor_of = factor_of * one(*cut)
    return factor_of


def normal_values(rng, extent, deviation, bound, split=(), kind=jnp.bfloat16):
    factor_of = steps_of(rng, extent, split, -0.22, 0.18) if split else 1.0
    drawn = jax.random.normal(rng, extent, jnp.float32) * deviation * factor_of
    return jnp.minimum(jnp.maximum(drawn, -bound), bound).astype(kind)


def setup_inputs(seed: int = 0) -> dict:
    key_list = jax.random.split(jax.random.key(seed), 8)
    query_act = draw_query_act(jax.random.fold_in(key_list[7], 71), 0)
    key_act = draw_key_act(jax.random.fold_in(key_list[7], 71), 0)
    value_act = normal_values(key_list[2], (TOKENS, D), 1.0, 6.0, ((0, 8), (1, 4)))
    out_weight = normal_values(key_list[3], (D, D), D ** -0.5, 0.125, ((0, 4),))
    cotangent = normal_values(key_list[4], (TOKENS, D), 1.0, 6.0, ((0, 8), (1, 4)))
    butterfly_cols = draw_butterfly_cols(jax.random.fold_in(key_list[7], 71), 0)
    global_cols = draw_global_cols(jax.random.fold_in(key_list[7], 71), 0)
    return {"query_act": query_act, "key_act": key_act, "value_act": value_act, "out_weight": out_weight, "cotangent": cotangent, "butterfly_cols": butterfly_cols, "global_cols": global_cols}


def reference(query_act, key_act, value_act, out_weight, cotangent, butterfly_cols, global_cols):
    factor = 1.0 / (HEAD_SIZE ** 0.5)
    key_span = (LEVELS + 1) * BLOCK + GLOBALS
    offsets = jnp.arange(BLOCK, dtype=jnp.int32)
    attn_grad = jnp.dot(cotangent, out_weight.T, preferred_element_type=jnp.float32).astype(jnp.bfloat16)

    def one_block(carry, index):
        key_sum, value_sum = carry
        block_ids = jnp.concatenate([index[None].astype(jnp.int32), butterfly_cols[index].astype(jnp.int32)])
        rows = (block_ids[:, None] * BLOCK + offsets[None, :]).reshape(-1)
        rows = jnp.concatenate([rows, global_cols.astype(jnp.int32)])
        start = index * BLOCK
        queries = lax.dynamic_slice_in_dim(query_act, start, BLOCK, 0).astype(jnp.float32).reshape(BLOCK, HEADS, HEAD_SIZE)
        grads_out = lax.dynamic_slice_in_dim(attn_grad, start, BLOCK, 0).astype(jnp.float32).reshape(BLOCK, HEADS, HEAD_SIZE)
        key_set = jnp.take(key_act, rows, axis=0).astype(jnp.float32).reshape(key_span, HEADS, HEAD_SIZE)
        value_set = jnp.take(value_act, rows, axis=0).astype(jnp.float32).reshape(key_span, HEADS, HEAD_SIZE)
        scores = jnp.einsum('qhd,khd->hqk', queries, key_set) * factor
        weights = jax.nn.softmax(scores, axis=-1)
        rounded = lax.optimization_barrier(weights.astype(jnp.bfloat16)).astype(jnp.float32)
        attention = jnp.einsum('hqk,khd->qhd', rounded, value_set).astype(jnp.bfloat16).reshape(BLOCK, D)
        prob_grad = jnp.einsum('qhd,khd->hqk', grads_out, value_set)
        delta = jnp.sum(weights * prob_grad, axis=-1, keepdims=True)
        score_grad = lax.optimization_barrier((weights * (prob_grad - delta)).astype(jnp.bfloat16)).astype(jnp.float32)
        query_part = (jnp.einsum('hqk,khd->qhd', score_grad, key_set) * factor).astype(jnp.bfloat16).reshape(BLOCK, D)
        key_part = jnp.einsum('hqk,qhd->khd', score_grad, queries) * factor
        value_part = jnp.einsum('hqk,qhd->khd', rounded, grads_out)
        key_sum = key_sum.at[rows].add(key_part.reshape(key_span, D))
        value_sum = value_sum.at[rows].add(value_part.reshape(key_span, D))
        return (key_sum, value_sum), (attention, query_part)

    start_sums = (jnp.zeros((TOKENS, D), jnp.float32), jnp.zeros((TOKENS, D), jnp.float32))
    (key_sum, value_sum), (attention, query_grad) = lax.scan(one_block, start_sums, jnp.arange(NBLK, dtype=jnp.int32))
    attention = attention.reshape(TOKENS, D)
    query_grad = query_grad.reshape(TOKENS, D)
    layer_out = jnp.dot(attention, out_weight, preferred_element_type=jnp.float32).astype(jnp.bfloat16)
    return (layer_out, query_grad, key_sum.astype(jnp.bfloat16), value_sum.astype(jnp.bfloat16))
```

```python
import functools
import math

import jax
import jax.numpy as jnp
from jax import lax
from jax.experimental import pallas as pl
from jax.experimental.pallas import tpu as pltpu
from jax.sharding import PartitionSpec as P

HEAD_SIZE = 128
BLOCK = 128
STAT_ROWS = 8


FACTOR = 1.0 / math.sqrt(HEAD_SIZE)
NT = (((1,), (1,)), ((), ()))
TN = (((0,), (0,)), ((), ()))
F32 = jnp.float32
BF16 = jnp.bfloat16


def swap(shard, axis, mask):
    return lax.ppermute(shard, axis, [(i, i ^ mask) for i in range(lax.axis_size(axis))])


def dot(a, b, dims=(((1,), (0,)), ((), ()))):
    return lax.dot_general(a, b, dims, preferred_element_type=F32)


def block_at(index):
    return pl.ds(pl.multiple_of(index * BLOCK, BLOCK), BLOCK)


def whole(shape):
    return pl.BlockSpec(shape, lambda h: (0,) * len(shape))


def by_head(rows):
    return pl.BlockSpec((rows, HEAD_SIZE), lambda h: (0, h))


SCALARS = pl.BlockSpec(memory_space=pltpu.SMEM)


def grad_kernel(head_axis, weight_ref, *refs):
    pieces, out_ref = refs[:-1], refs[-1]
    width = pieces[0].shape[1]
    mine = lax.axis_index(head_axis)
    total = None
    for m, piece in enumerate(pieces):
        start = pl.multiple_of(jnp.bitwise_xor(mine, m) * width, width)
        part = dot(piece[...], weight_ref[:, pl.ds(start, width)], NT)
        total = part if total is None else total + part
    out_ref[...] = total.astype(BF16)


def attn_grad_of(pieces, weight):
    return pl.pallas_call(
        functools.partial(grad_kernel, "head"),
        out_shape=jax.ShapeDtypeStruct(pieces[0].shape, BF16),
        name="attn_grad",
    )(weight, *pieces)


def project_kernel(head_axis, att_ref, weight_ref, own_ref, *outs):
    width = own_ref.shape[1]
    mine = lax.axis_index(head_axis)
    for m, out in enumerate((own_ref,) + outs):
        start = pl.multiple_of(jnp.bitwise_xor(mine, m) * width, width)
        out[...] = dot(att_ref[...], weight_ref[:, pl.ds(start, width)]).astype(out.dtype)


def project(attention, weight, groups):
    rows = attention.shape[0]
    width = weight.shape[1] // groups
    shapes = [jax.ShapeDtypeStruct((rows, width), F32 if m == 0 else BF16) for m in range(groups)]
    return pl.pallas_call(
        functools.partial(project_kernel, "head"), out_shape=shapes, name="project"
    )(attention, weight)


def select_kernel(masks, ctx_axis, cols_ref, *refs):
    count = len(masks)
    keys, values = refs[:count], refs[count : 2 * count]
    out_keys, out_values = refs[2 * count :]
    rows = keys[0].shape[0]
    device = lax.axis_index(ctx_axis)
    slots = cols_ref.shape[1]
    row_ids = lax.broadcasted_iota(jnp.int32, (rows, slots), 0)
    key_sum, value_sum = None, None
    for t, mask in enumerate(masks):
        local = cols_ref[...] - jnp.bitwise_xor(device, mask) * rows
        chosen = (row_ids == local).astype(F32).astype(BF16)
        key_part = dot(chosen, keys[t][...], TN)
        value_part = dot(chosen, values[t][...], TN)
        key_sum = key_part if t == 0 else key_sum + key_part
        value_sum = value_part if t == 0 else value_sum + value_part
    out_keys[...] = key_sum.astype(BF16)
    out_values[...] = value_sum.astype(BF16)


def select_globals(masks, cols, keys, values):
    rows, width = keys[0].shape
    slots = cols.shape[1]
    shape = jax.ShapeDtypeStruct((slots, width), BF16)
    return pl.pallas_call(
        functools.partial(select_kernel, masks, "ctx"),
        grid=(width // HEAD_SIZE,),
        in_specs=[whole(cols.shape)] + [by_head(rows)] * (2 * len(masks)),
        out_specs=[by_head(slots)] * 2,
        out_shape=[shape, shape],
        name="select_globals",
    )(cols, *keys, *values)


def query_kernel(strides, glob_parts, ctx_axis, cols_ref, *refs):
    query, grad, own_key, own_value = refs[:4]
    refs = refs[4:]
    far_keys, far_values, refs = refs[:strides], refs[strides : 2 * strides], refs[2 * strides :]
    glob_keys, glob_values = refs[:glob_parts], refs[glob_parts : 2 * glob_parts]
    att_out, query_out, keep_out, send_out, stat_out, stats = refs[2 * glob_parts :]
    blocks = query.shape[0] // BLOCK
    near = (strides + 1) * BLOCK
    head, heads = pl.program_id(0), pl.num_programs(0)
    device = lax.axis_index(ctx_axis)
    glob_key = sum((ref[...] for ref in glob_keys[1:]), glob_keys[0][...])
    glob_value = sum((ref[...] for ref in glob_values[1:]), glob_values[0][...])
    lane = lax.broadcasted_iota(jnp.int32, (BLOCK, BLOCK), 1)
    glob_grads, glob_weights = [], []
    for i in range(blocks):
        rows = pl.ds(i * BLOCK, BLOCK)
        picks = [
            block_at(
                cols_ref[device * blocks + i, s] - jnp.bitwise_xor(device, 1 << s) * blocks
            )
            for s in range(strides)
        ]
        keys = jnp.concatenate(
            [own_key[rows, :]] + [far_keys[s][picks[s], :] for s in range(strides)] + [glob_key], 0
        )
        values = jnp.concatenate(
            [own_value[rows, :]]
            + [far_values[s][picks[s], :] for s in range(strides)]
            + [glob_value],
            0,
        )
        scores = dot(query[rows, :], keys, NT) * FACTOR
        top = jnp.max(scores, axis=1, keepdims=True)
        exponent = jnp.exp(scores - top)
        scale = 1.0 / jnp.sum(exponent, axis=1, keepdims=True)
        weights = exponent * scale
        rounded = weights.astype(BF16)
        att_out[rows, :] = dot(rounded, values).astype(BF16)
        prob_grad = dot(grad[rows, :], values, NT)
        delta = jnp.sum(weights * prob_grad, axis=1, keepdims=True)
        score_grad = (weights * (prob_grad - delta)).astype(BF16)
        query_out[rows, :] = (dot(score_grad, keys) * FACTOR).astype(BF16)
        glob_grads.append(score_grad[:, near:])
        glob_weights.append(rounded[:, near:])
        held = stats[rows, :]
        for place, column in enumerate((top, scale, delta)):
            held = jnp.where(lane == head * STAT_ROWS + place, column, held)
        stats[rows, :] = held
    key_term = dot(jnp.concatenate(glob_grads, 0), query[...], TN)
    value_term = dot(jnp.concatenate(glob_weights, 0), grad[...], TN)
    odd = jnp.bitwise_and(device, 1) == 1
    keep_out[...] = jnp.where(odd, value_term, key_term)
    send_out[...] = jnp.where(odd, key_term, value_term).astype(BF16)

    @pl.when(head == heads - 1)
    def _():
        for i in range(blocks):
            rows = pl.ds(i * BLOCK, BLOCK)
            stat_out[:, rows] = stats[rows, :].T[: stat_out.shape[0]]


def query_side(cols, query, grad, key, value, far_keys, far_values, glob_keys, glob_values):
    rows, width = query.shape
    heads = width // HEAD_SIZE
    strides = len(far_keys)
    slots = glob_keys[0].shape[0]
    stat_rows = heads * STAT_ROWS
    return pl.pallas_call(
        functools.partial(query_kernel, strides, len(glob_keys), "ctx"),
        grid=(heads,),
        in_specs=[SCALARS]
        + [by_head(rows)] * (4 + 2 * strides)
        + [by_head(slots)] * (2 * len(glob_keys)),
        out_specs=[by_head(rows)] * 2 + [by_head(slots)] * 2 + [whole((stat_rows, rows))],
        out_shape=[
            jax.ShapeDtypeStruct((rows, width), BF16),
            jax.ShapeDtypeStruct((rows, width), BF16),
            jax.ShapeDtypeStruct((slots, width), F32),
            jax.ShapeDtypeStruct((slots, width), BF16),
            jax.ShapeDtypeStruct((stat_rows, rows), F32),
        ],
        scratch_shapes=[pltpu.VMEM((rows, BLOCK), F32)],
        name="query_side",
    )(cols, query, grad, key, value, *far_keys, *far_values, *glob_keys, *glob_values)


def key_kernel(strides, ctx_axis, cols_ref, key, value, *refs):
    sources = strides + 1
    queries, grads, stats = refs[:sources], refs[sources : 2 * sources], refs[2 * sources : 3 * sources]
    key_out, value_out = refs[3 * sources :]
    blocks = key.shape[0] // BLOCK
    device = lax.axis_index(ctx_axis)
    for s in range(-1, strides):
        for i in range(blocks):
            rows = pl.ds(i * BLOCK, BLOCK)
            if s < 0:
                place = rows
            else:
                partner = jnp.bitwise_xor(device, 1 << s)
                place = block_at(cols_ref[partner * blocks + i, s] - device * blocks)
            q, g = queries[s + 1][rows, :], grads[s + 1][rows, :]
            top, scale, delta = (
                stats[s + 1][part : part + 1, rows] for part in range(3)
            )
            weights = jnp.exp(dot(key[place, :], q, NT) * FACTOR - top) * scale
            prob_grad = dot(value[place, :], g, NT)
            score_grad = (weights * (prob_grad - delta)).astype(BF16)
            key_term = dot(score_grad, q)
            value_term = dot(weights.astype(BF16), g)
            if s < 0:
                key_out[place, :] = key_term
                value_out[place, :] = value_term
            else:
                key_out[place, :] += key_term
                value_out[place, :] += value_term


def key_side(cols, key, value, queries, grads, stats):
    rows, width = key.shape
    strides = len(queries) - 1
    shape = jax.ShapeDtypeStruct((rows, width), F32)
    return pl.pallas_call(
        functools.partial(key_kernel, strides, "ctx"),
        grid=(width // HEAD_SIZE,),
        in_specs=[SCALARS]
        + [by_head(rows)] * (2 + 2 * (strides + 1))
        + [pl.BlockSpec((STAT_ROWS, rows), lambda h: (h, 0))] * (strides + 1),
        out_specs=[by_head(rows)] * 2,
        out_shape=[shape, shape],
        name="key_side",
    )(cols, key, value, *queries, *grads, *stats)


def final_kernel(ctx_axis, cols_ref, key, value, kept, got, key_out, value_out):
    rows, slots = key.shape[0], kept.shape[0]
    device = lax.axis_index(ctx_axis)
    row_ids = lax.broadcasted_iota(jnp.int32, (rows, slots), 0)
    chosen = (row_ids == cols_ref[...] - device * rows).astype(F32).astype(BF16)
    odd = jnp.bitwise_and(device, 1) == 1
    glob_key = jnp.where(odd, got[...].astype(F32), kept[...].astype(F32)).astype(BF16)
    glob_value = jnp.where(odd, kept[...].astype(F32), got[...].astype(F32)).astype(BF16)
    key_out[...] = ((key[...] + dot(chosen, glob_key)) * FACTOR).astype(BF16)
    value_out[...] = (value[...] + dot(chosen, glob_value)).astype(BF16)


def finish(cols, key, value, kept, got):
    rows, width = key.shape
    slots = kept.shape[0]
    shape = jax.ShapeDtypeStruct((rows, width), BF16)
    return pl.pallas_call(
        functools.partial(final_kernel, "ctx"),
        grid=(width // HEAD_SIZE,),
        in_specs=[whole(cols.shape)] + [by_head(rows)] * 2 + [by_head(slots)] * 2,
        out_specs=[by_head(rows)] * 2,
        out_shape=[shape, shape],
        name="finish",
    )(cols, key, value, kept, got)


def ring_gather(first, second):
    near = {m: (swap(first, "ctx", m), swap(second, "ctx", m)) for m in (2, 6)}
    near[1] = (swap(first, "ctx", 1), swap(second, "ctx", 1))
    near[4] = (swap(near[6][0], "ctx", 2), swap(near[2][1], "ctx", 6))
    return near


def direct_gather(first, second, strides):
    return {1 << s: (swap(first, "ctx", 1 << s), swap(second, "ctx", 1 << s)) for s in range(strides)}


def ring_reduce(keep, send):
    total = keep + swap(send, "ctx", 1)
    half = total.shape[0] // 2
    parts = []
    for part, order in ((total[:half], (2, 6)), (total[half:], (6, 2))):
        for mask in order:
            part = part + swap(part.astype(BF16), "ctx", mask).astype(F32)
        parts.append(part.astype(BF16))
    kept = jnp.concatenate(parts, 0)
    return kept, swap(kept, "ctx", 1)


def per_device(query_act, key_act, value_act, out_weight, cotangent, butterfly_cols, global_cols):
    strides = butterfly_cols.shape[1]
    groups = lax.axis_size("head")
    ring = strides == 3 and lax.axis_size("ctx") == 1 << strides
    cols = global_cols.reshape(1, -1)
    masks = [1 << s for s in range(strides)]

    gather = ring_gather if ring else functools.partial(direct_gather, strides=strides)
    near = gather(key_act, value_act)
    pieces = [cotangent] + [swap(cotangent, "head", m) for m in range(1, groups)]
    attn_grad = attn_grad_of(pieces, out_weight)
    if ring:
        held = (0, 2, 6, 4)
        near[0] = (key_act, value_act)
        glob_key, glob_value = select_globals(
            held, cols, [near[m][0] for m in held], [near[m][1] for m in held]
        )
        glob_keys = [glob_key, swap(glob_key, "ctx", 1)]
        glob_values = [glob_value, swap(glob_value, "ctx", 1)]
    else:
        glob_keys, glob_values = (
            [part] for part in lax.psum(select_globals((0,), cols, [key_act], [value_act]), "ctx")
        )
    far_queries = gather(query_act, attn_grad)
    attention, query_grad, keep, send, stats = query_side(
        butterfly_cols,
        query_act,
        attn_grad,
        key_act,
        value_act,
        [near[m][0] for m in masks],
        [near[m][1] for m in masks],
        glob_keys,
        glob_values,
    )
    far_stats = [swap(stats, "ctx", m) for m in masks]
    if ring:
        kept, got = ring_reduce(keep, send)
    else:
        odd = jnp.bitwise_and(lax.axis_index("ctx"), 1) == 1
        send = send.astype(F32)
        key_term, value_term = lax.psum(
            (jnp.where(odd, send, keep), jnp.where(odd, keep, send)), "ctx"
        )
        kept = jnp.where(odd, value_term, key_term).astype(BF16)
        got = jnp.where(odd, key_term, value_term).astype(BF16)
    terms = project(attention, out_weight, groups)
    layer_out = terms[0]
    for m in range(1, groups):
        layer_out = layer_out + swap(terms[m], "head", m).astype(F32)
    key_sum, value_sum = key_side(
        butterfly_cols,
        key_act,
        value_act,
        [query_act] + [far_queries[m][0] for m in masks],
        [attn_grad] + [far_queries[m][1] for m in masks],
        [stats] + far_stats,
    )
    key_grad, value_grad = finish(cols, key_sum, value_sum, kept, got)
    return (layer_out.astype(BF16), query_grad, key_grad, value_grad)


def solution(mesh):
    in_specs = (
        P("ctx", "head"),
        P("ctx", "head"),
        P("ctx", "head"),
        P("head", None),
        P("ctx", "head"),
        P(),
        P(),
    )
    out_specs = (P("ctx", "head"),) * 4
    return jax.shard_map(
        per_device, mesh=mesh, in_specs=in_specs, out_specs=out_specs, check_vma=False
    )
```

```python
import functools
import math

import jax
import jax.numpy as jnp
from jax import lax
from jax.experimental import pallas as pl
from jax.experimental.pallas import tpu as pltpu
from jax.sharding import PartitionSpec as P


HEAD_SIZE = 128
BLOCK = 128
STAT_ROWS = 8


FACTOR = 1.0 / math.sqrt(HEAD_SIZE)
NT = (((1,), (1,)), ((), ()))
TN = (((0,), (0,)), ((), ()))
F32 = jnp.float32
BF16 = jnp.bfloat16


def swap(shard, axis, mask):
    return lax.ppermute(shard, axis, [(i, i ^ mask) for i in range(lax.axis_size(axis))])


def call(kernel, out_shape, *operands, scalars=0, scratch=()):
    in_specs = [pl.BlockSpec(memory_space=pltpu.SMEM)] * scalars
    in_specs += [pl.BlockSpec(memory_space=pltpu.VMEM)] * (len(operands) - scalars)
    outs = jax.tree.map(lambda _: pl.BlockSpec(memory_space=pltpu.VMEM), out_shape)
    return pl.pallas_call(
        kernel, in_specs=in_specs, out_specs=outs, out_shape=out_shape, scratch_shapes=scratch
    )(*operands)


def like(shape, dtype=jnp.bfloat16):
    return jax.ShapeDtypeStruct(shape, dtype)


def dot(a, b, dims=(((1,), (0,)), ((), ()))):
    return lax.dot_general(a, b, dims, preferred_element_type=F32)


def block_at(index):
    return pl.ds(pl.multiple_of(index * BLOCK, BLOCK), BLOCK)


def columns_of(head):
    return pl.ds(pl.multiple_of(head * HEAD_SIZE, HEAD_SIZE), HEAD_SIZE)


def grad_kernel(weight_ref, *refs):
    pieces, out_ref = refs[:-1], refs[-1]
    width = pieces[0].shape[1]
    mine = lax.axis_index("head")
    total = None
    for m, piece in enumerate(pieces):
        start = pl.multiple_of(jnp.bitwise_xor(mine, m) * width, width)
        part = dot(piece[...], weight_ref[:, pl.ds(start, width)], NT)
        total = part if total is None else total + part
    out_ref[...] = total.astype(BF16)


def project_kernel(att_ref, weight_ref, *outs):
    width = outs[0].shape[1]
    mine = lax.axis_index("head")
    for m, out in enumerate(outs):
        start = pl.multiple_of(jnp.bitwise_xor(mine, m) * width, width)
        out[...] = dot(att_ref[...], weight_ref[:, pl.ds(start, width)]).astype(out.dtype)


def hot_kernel(masks, cols_ref, scatter_ref, *select_refs):
    rows, slots = scatter_ref.shape
    device = lax.axis_index("ctx")
    row_ids = lax.broadcasted_iota(jnp.int32, (rows, slots), 0)
    for mask, select_ref in zip(masks, select_refs):
        local = cols_ref[...] - jnp.bitwise_xor(device, mask) * rows
        chosen = (row_ids == local).astype(F32)
        if mask == 0:
            scatter_ref[...] = chosen.astype(BF16)
        select_ref[...] = chosen.T.astype(BF16)


def select_kernel(count, more, *refs):
    selects, keys, values = (refs[part * count : (part + 1) * count] for part in range(3))
    refs = refs[3 * count :]
    outs = refs[-2:]
    for sources, so_far, out in zip((keys, values), refs[:-2] if more else (None, None), outs):
        total = so_far[...].astype(F32) if more else 0.0
        for select, source in zip(selects, sources):
            total = total + dot(select[...], source[...])
        out[...] = total.astype(BF16)


def select_globals(selects, keys, values, so_far=()):
    shape = like((selects[0].shape[0], keys[0].shape[1]))
    kernel = functools.partial(select_kernel, len(selects), bool(so_far))
    return call(kernel, [shape, shape], *selects, *keys, *values, *so_far)


def query_kernel(strides, glob_parts, cols_ref, *refs):
    query, grad, own_key, own_value = refs[:4]
    refs = refs[4:]
    far_keys, far_values, refs = refs[:strides], refs[strides : 2 * strides], refs[2 * strides :]
    glob_keys, glob_values = refs[:glob_parts], refs[glob_parts : 2 * glob_parts]
    att_out, query_out, keep_out, send_out, stat_out, stats = refs[2 * glob_parts :]
    blocks = query.shape[0] // BLOCK
    heads = query.shape[1] // HEAD_SIZE
    near = (strides + 1) * BLOCK
    device = lax.axis_index("ctx")
    odd = jnp.bitwise_and(device, 1) == 1
    lane = lax.broadcasted_iota(jnp.int32, (BLOCK, BLOCK), 1)

    def one_head(head, _):
        part = columns_of(head)
        glob_key = sum((ref[:, part] for ref in glob_keys[1:]), glob_keys[0][:, part])
        glob_value = sum((ref[:, part] for ref in glob_values[1:]), glob_values[0][:, part])
        glob_grads, glob_weights = [], []
        for i in range(blocks):
            rows = pl.ds(i * BLOCK, BLOCK)
            picks = [
                block_at(
                    cols_ref[s, device * blocks + i] - jnp.bitwise_xor(device, 1 << s) * blocks
                )
                for s in range(strides)
            ]
            keys = jnp.concatenate(
                [own_key[rows, part]]
                + [far_keys[s][picks[s], part] for s in range(strides)]
                + [glob_key],
                0,
            )
            values = jnp.concatenate(
                [own_value[rows, part]]
                + [far_values[s][picks[s], part] for s in range(strides)]
                + [glob_value],
                0,
            )
            scores = dot(query[rows, part], keys, NT) * FACTOR
            top = jnp.max(scores, axis=1, keepdims=True)
            exponent = jnp.exp(scores - top)
            scale = 1.0 / jnp.sum(exponent, axis=1, keepdims=True)
            weights = exponent * scale
            rounded = weights.astype(BF16)
            att_out[rows, part] = dot(rounded, values).astype(BF16)
            prob_grad = dot(grad[rows, part], values, NT)
            delta = jnp.sum(weights * prob_grad, axis=1, keepdims=True)
            score_grad = (weights * (prob_grad - delta)).astype(BF16)
            query_out[rows, part] = (dot(score_grad, keys) * FACTOR).astype(BF16)
            glob_grads.append(score_grad[:, near:])
            glob_weights.append(rounded[:, near:])
            held = stats[rows, :]
            for place, column in enumerate((top, scale, delta)):
                held = jnp.where(lane == head * STAT_ROWS + place, column, held)
            stats[rows, :] = held
        key_term = dot(jnp.concatenate(glob_grads, 0), query[:, part], TN)
        value_term = dot(jnp.concatenate(glob_weights, 0), grad[:, part], TN)
        keep_out[:, part] = jnp.where(odd, value_term, key_term)
        send_out[:, part] = jnp.where(odd, key_term, value_term).astype(BF16)

    lax.fori_loop(0, heads, one_head, None)
    for i in range(blocks):
        rows = pl.ds(i * BLOCK, BLOCK)
        stat_out[:, rows] = stats[rows, :].T[: stat_out.shape[0]]


def query_side(cols, query, grad, key, value, far_keys, far_values, glob_keys, glob_values):
    rows, width = query.shape
    strides = len(far_keys)
    slots = glob_keys[0].shape[0]
    shapes = [
        like((rows, width)),
        like((rows, width)),
        like((slots, width), F32),
        like((slots, width)),
        like((width // HEAD_SIZE * STAT_ROWS, rows), F32),
    ]
    return call(
        functools.partial(query_kernel, strides, len(glob_keys)),
        shapes,
        cols,
        query,
        grad,
        key,
        value,
        *far_keys,
        *far_values,
        *glob_keys,
        *glob_values,
        scalars=1,
        scratch=[pltpu.VMEM((rows, BLOCK), F32)],
    )


def key_kernel(sources, cols_ref, key, value, *refs):
    count = len(sources)
    queries, grads, stats = (refs[part * count : (part + 1) * count] for part in range(3))
    so_far, (key_out, value_out) = refs[3 * count : -2], refs[-2:]
    blocks = key.shape[0] // BLOCK
    heads = key.shape[1] // HEAD_SIZE
    device = lax.axis_index("ctx")

    def one_head(head, _):
        part = columns_of(head)
        stat_at = pl.multiple_of(head * STAT_ROWS, STAT_ROWS)
        if so_far:
            key_out[:, part] = so_far[0][:, part]
            value_out[:, part] = so_far[1][:, part]
        for at, s in enumerate(sources):
            for i in range(blocks):
                rows = pl.ds(i * BLOCK, BLOCK)
                if s < 0:
                    place = rows
                else:
                    partner = jnp.bitwise_xor(device, 1 << s)
                    place = block_at(cols_ref[s, partner * blocks + i] - device * blocks)
                q, g = queries[at][rows, part], grads[at][rows, part]
                stat = stats[at][pl.ds(stat_at, STAT_ROWS), rows]
                top, scale, delta = stat[0:1], stat[1:2], stat[2:3]
                weights = jnp.exp(dot(key[place, part], q, NT) * FACTOR - top) * scale
                prob_grad = dot(value[place, part], g, NT)
                score_grad = (weights * (prob_grad - delta)).astype(BF16)
                key_term = dot(score_grad, q)
                value_term = dot(weights.astype(BF16), g)
                if s < 0:
                    key_out[place, part] = key_term
                    value_out[place, part] = value_term
                else:
                    key_out[place, part] += key_term
                    value_out[place, part] += value_term

    lax.fori_loop(0, heads, one_head, None)


def key_side(sources, cols, key, value, queries, grads, stats, so_far=()):
    shape = like(key.shape, F32)
    return call(
        functools.partial(key_kernel, sources),
        [shape, shape],
        cols,
        key,
        value,
        *queries,
        *grads,
        *stats,
        *so_far,
        scalars=1,
    )


def final_kernel(scatter, key, value, kept, got, key_out, value_out):
    odd = jnp.bitwise_and(lax.axis_index("ctx"), 1) == 1
    kept_rows = dot(scatter[...], kept[...])
    got_rows = dot(scatter[...], got[...])
    key_rows = jnp.where(odd, got_rows, kept_rows)
    value_rows = jnp.where(odd, kept_rows, got_rows)
    key_out[...] = ((key[...] + key_rows) * FACTOR).astype(BF16)
    value_out[...] = (value[...] + value_rows).astype(BF16)


def finish(scatter, key, value, kept, got):
    rows, width = key.shape
    slots = kept.shape[0]
    part = lambda count: pl.BlockSpec((count, width // 2), lambda h: (0, h))
    shape = like((rows, width))
    return pl.pallas_call(
        final_kernel,
        grid=(2,),
        in_specs=[pl.BlockSpec((rows, slots), lambda h: (0, 0))]
        + [part(rows)] * 2
        + [part(slots)] * 2,
        out_specs=[part(rows)] * 2,
        out_shape=[shape, shape],
        name="finish",
    )(scatter, key, value, kept, got)


def per_device(query_act, key_act, value_act, out_weight, cotangent, butterfly_cols, global_cols):
    strides = butterfly_cols.shape[1]
    groups = lax.axis_size("head")
    ring = strides == 3 and lax.axis_size("ctx") == 1 << strides
    cols = butterfly_cols.T
    slots = global_cols.shape[0]
    rows, width = key_act.shape
    masks = [1 << s for s in range(strides)]
    held = (0, 2, 6, 4) if ring else (0,)

    scatter, *selects = call(
        functools.partial(hot_kernel, held),
        [like((rows, slots))] + [like((slots, rows))] * len(held),
        global_cols.reshape(1, -1),
    )
    direct = (2, 6, 1) if ring else masks
    near = {m: (swap(key_act, "ctx", m), swap(value_act, "ctx", m)) for m in direct}
    pieces = [cotangent] + [swap(cotangent, "head", m) for m in range(1, groups)]
    near[0] = (key_act, value_act)
    if ring:
        near[4] = (swap(near[6][0], "ctx", 2), swap(near[2][1], "ctx", 6))
        first, last = held[:-1], held[-1]
        so_far = select_globals(
            selects[:-1], [near[m][0] for m in first], [near[m][1] for m in first]
        )
        glob_key, glob_value = select_globals(
            selects[-1:], [near[last][0]], [near[last][1]], so_far
        )
        glob_keys = [glob_key, swap(glob_key, "ctx", 1)]
        glob_values = [glob_value, swap(glob_value, "ctx", 1)]
    else:
        parts = select_globals(selects, [key_act], [value_act])
        glob_keys, glob_values = ([part] for part in lax.psum(tuple(parts), "ctx"))
    far_query = {m: swap(query_act, "ctx", m) for m in masks}
    attn_grad = call(grad_kernel, like((rows, width)), out_weight, *pieces)
    far_grad = {m: swap(attn_grad, "ctx", m) for m in masks}
    attention, query_grad, keep, send, stats = query_side(
        cols,
        query_act,
        attn_grad,
        key_act,
        value_act,
        [near[m][0] for m in masks],
        [near[m][1] for m in masks],
        glob_keys,
        glob_values,
    )
    far_stats = {m: swap(stats, "ctx", m) for m in masks}
    if ring:
        total = keep + swap(send, "ctx", 1).astype(F32)
        total = total + swap(total.astype(BF16), "ctx", 2).astype(F32)
        total = total + swap(total.astype(BF16), "ctx", 6).astype(F32)
        kept = total.astype(BF16)
        got = swap(kept, "ctx", 1)
    else:
        odd = jnp.bitwise_and(lax.axis_index("ctx"), 1) == 1
        send = send.astype(F32)
        key_term, value_term = lax.psum(
            (jnp.where(odd, send, keep), jnp.where(odd, keep, send)), "ctx"
        )
        kept = jnp.where(odd, value_term, key_term).astype(BF16)
        got = jnp.where(odd, key_term, value_term).astype(BF16)
    term = out_weight.shape[1] // groups
    shapes = [like((rows, term), F32 if m == 0 else BF16) for m in range(groups)]
    terms = call(project_kernel, shapes, attention, out_weight)
    layer_out = terms[0]
    for m in range(1, groups):
        layer_out = layer_out + swap(terms[m], "head", m).astype(F32)
    so_far = key_side((-1,), cols, key_act, value_act, [query_act], [attn_grad], [stats])
    key_sum, value_sum = key_side(
        tuple(range(strides)),
        cols,
        key_act,
        value_act,
        [far_query[m] for m in masks],
        [far_grad[m] for m in masks],
        [far_stats[m] for m in masks],
        so_far,
    )
    key_grad, value_grad = finish(scatter, key_sum, value_sum, kept, got)
    return (layer_out.astype(BF16), query_grad, key_grad, value_grad)


def solution(mesh):
    in_specs = (
        P("ctx", "head"),
        P("ctx", "head"),
        P("ctx", "head"),
        P("head", None),
        P("ctx", "head"),
        P(),
        P(),
    )
    out_specs = (P("ctx", "head"),) * 4

    return jax.shard_map(
        per_device, mesh=mesh, in_specs=in_specs, out_specs=out_specs, check_vma=False
    )
```

```python
import functools
import math

import jax
import jax.numpy as jnp
from jax import lax
from jax.experimental import pallas as pl
from jax.experimental.pallas import tpu as pltpu
from jax.sharding import PartitionSpec as P


HEAD_SIZE = 128
BLOCK = 128
STAT_ROWS = 8
KERNEL_VMEM = 16 * 2**20


FACTOR = 1.0 / math.sqrt(HEAD_SIZE)
NT = (((1,), (1,)), ((), ()))
TN = (((0,), (0,)), ((), ()))
F32 = jnp.float32
BF16 = jnp.bfloat16


def swap(shard, axis, mask):
    return lax.ppermute(shard, axis, [(i, i ^ mask) for i in range(lax.axis_size(axis))])


def call(kernel, out_shape, *operands, scalars=0, scratch=()):
    in_specs = [pl.BlockSpec(memory_space=pltpu.SMEM)] * scalars
    in_specs += [pl.BlockSpec(memory_space=pltpu.VMEM)] * (len(operands) - scalars)
    outs = [pl.BlockSpec(memory_space=pltpu.VMEM)] * len(out_shape)
    placed = [pltpu.with_memory_space_constraint(o, pltpu.VMEM) for o in operands[scalars:]]
    return pl.pallas_call(
        kernel,
        in_specs=in_specs,
        out_specs=outs,
        out_shape=out_shape,
        scratch_shapes=scratch,
        compiler_params=pltpu.CompilerParams(vmem_limit_bytes=KERNEL_VMEM),
    )(*operands[:scalars], *placed)


def like(shape, dtype=jnp.bfloat16):
    return pltpu.VMEM(shape, dtype)


def dot(a, b, dims=(((1,), (0,)), ((), ()))):
    return lax.dot_general(a, b, dims, preferred_element_type=F32)


def block_at(index):
    return pl.ds(pl.multiple_of(index * BLOCK, BLOCK), BLOCK)


def columns_of(head):
    return pl.ds(pl.multiple_of(head * HEAD_SIZE, HEAD_SIZE), HEAD_SIZE)


def grad_kernel(weight_ref, *refs):
    pieces, out_ref = refs[:-1], refs[-1]
    width = pieces[0].shape[1]
    mine = lax.axis_index("head")
    total = None
    for m, piece in enumerate(pieces):
        start = pl.multiple_of(jnp.bitwise_xor(mine, m) * width, width)
        part = dot(piece[...], weight_ref[:, pl.ds(start, width)], NT)
        total = part if total is None else total + part
    out_ref[...] = total.astype(BF16)


def project_kernel(att_ref, weight_ref, *outs):
    width = outs[0].shape[1]
    mine = lax.axis_index("head")
    for m, out in enumerate(outs):
        start = pl.multiple_of(jnp.bitwise_xor(mine, m) * width, width)
        out[...] = dot(att_ref[...], weight_ref[:, pl.ds(start, width)]).astype(out.dtype)


def hot_kernel(masks, groups, cols_ref, scatter_ref, *outs):
    rows, slots = scatter_ref.shape
    device = lax.axis_index("ctx")
    row_ids = lax.broadcasted_iota(jnp.int32, (rows, slots), 0)

    def local(mask):
        return cols_ref[...] - jnp.bitwise_xor(device, mask) * rows

    for mask, out in zip(masks, outs):
        chosen = (row_ids == local(mask)).astype(F32)
        if mask == 0:
            scatter_ref[...] = chosen.astype(BF16)
        out[...] = chosen.T.astype(BF16)
    for group, out in zip(groups, outs[len(masks) :]):
        owned = 0.0
        for mask in group:
            at = jnp.broadcast_to(local(mask), (out.shape[1], slots))
            owned = owned + jnp.logical_and(at >= 0, at < rows).astype(F32)
        out[...] = owned.T


def select_kernel(count, *refs):
    total = dot(refs[0][...], refs[count][...])
    for select, source in zip(refs[1:count], refs[count + 1 : -1]):
        total = total + dot(select[...], source[...])
    refs[-1][...] = total.astype(BF16)


def select_globals(selects, sources):
    shape = like((selects[0].shape[0], sources[0].shape[1]))
    kernel = functools.partial(select_kernel, len(selects))
    return call(kernel, [shape], *selects, *sources)[0]


def merged(have, got, owned):
    return (have.astype(F32) + owned * got.astype(F32)).astype(BF16)


def merge_kernel(have, got, owned, out):
    for start in range(0, out.shape[1], HEAD_SIZE):
        part = pl.ds(start, HEAD_SIZE)
        out[:, part] = merged(have[:, part], got[:, part], owned[...])


def merge(have, got, owned):
    return call(merge_kernel, [like(have.shape)], have, got, owned)[0]


def query_kernel(strides, glob_parts, cols_ref, *refs):
    query, grad, own_key, own_value = refs[:4]
    refs = refs[4:]
    far_keys, far_values, refs = refs[:strides], refs[strides : 2 * strides], refs[2 * strides :]
    glob_keys, glob_values = refs[:glob_parts], refs[glob_parts : 2 * glob_parts]
    att_out, query_out, keep_out, send_out, stat_out, stats = refs[-6:]
    blocks = query.shape[0] // BLOCK
    heads = query.shape[1] // HEAD_SIZE
    near = (strides + 1) * BLOCK
    device = lax.axis_index("ctx")
    odd = jnp.bitwise_and(device, 1) == 1
    lane = lax.broadcasted_iota(jnp.int32, (BLOCK, BLOCK), 1)

    def one_head(head, _):
        part = columns_of(head)
        if glob_parts == 1:
            glob_key, glob_value = glob_keys[0][:, part], glob_values[0][:, part]
        else:
            owned = refs[2 * glob_parts][...]
            glob_key, glob_value = (
                merged(have[:, part], got[:, part], owned)
                for have, got in (glob_keys, glob_values)
            )
        glob_grads, glob_weights = [], []
        for i in range(blocks):
            rows = pl.ds(i * BLOCK, BLOCK)
            picks = [
                block_at(
                    cols_ref[s, device * blocks + i] - jnp.bitwise_xor(device, 1 << s) * blocks
                )
                for s in range(strides)
            ]
            keys = jnp.concatenate(
                [own_key[rows, part]]
                + [far_keys[s][picks[s], part] for s in range(strides)]
                + [glob_key],
                0,
            )
            values = jnp.concatenate(
                [own_value[rows, part]]
                + [far_values[s][picks[s], part] for s in range(strides)]
                + [glob_value],
                0,
            )
            scores = dot(query[rows, part], keys, NT) * FACTOR
            top = jnp.max(scores, axis=1, keepdims=True)
            exponent = jnp.exp(scores - top)
            scale = 1.0 / jnp.sum(exponent, axis=1, keepdims=True)
            weights = exponent * scale
            rounded = weights.astype(BF16)
            att_out[rows, part] = dot(rounded, values).astype(BF16)
            prob_grad = dot(grad[rows, part], values, NT)
            delta = jnp.sum(weights * prob_grad, axis=1, keepdims=True)
            score_grad = (weights * (prob_grad - delta)).astype(BF16)
            query_out[rows, part] = (dot(score_grad, keys) * FACTOR).astype(BF16)
            glob_grads.append(score_grad[:, near:])
            glob_weights.append(rounded[:, near:])
            held = stats[rows, :]
            for place, column in enumerate((top, scale, delta)):
                held = jnp.where(lane == head * STAT_ROWS + place, column, held)
            stats[rows, :] = held
        key_term = dot(jnp.concatenate(glob_grads, 0), query[:, part], TN)
        value_term = dot(jnp.concatenate(glob_weights, 0), grad[:, part], TN)
        keep_out[:, part] = jnp.where(odd, value_term, key_term)
        send_out[:, part] = jnp.where(odd, key_term, value_term).astype(BF16)

    lax.fori_loop(0, heads, one_head, None)
    for i in range(blocks):
        rows = pl.ds(i * BLOCK, BLOCK)
        stat_out[:, rows] = stats[rows, :].T[: stat_out.shape[0]]


def query_side(
    cols, query, grad, key, value, far_keys, far_values, glob_keys, glob_values, owned=()
):
    rows, width = query.shape
    strides = len(far_keys)
    slots = glob_keys[0].shape[0]
    shapes = [
        like((rows, width)),
        like((rows, width)),
        like((slots, width), F32),
        like((slots, width)),
        like((width // HEAD_SIZE * STAT_ROWS, rows), F32),
    ]
    return call(
        functools.partial(query_kernel, strides, len(glob_keys)),
        shapes,
        cols,
        query,
        grad,
        key,
        value,
        *far_keys,
        *far_values,
        *glob_keys,
        *glob_values,
        *owned,
        scalars=1,
        scratch=[pltpu.VMEM((rows, BLOCK), F32)],
    )


def key_kernel(sources, cols_ref, key, value, *refs):
    count = len(sources)
    queries, grads, stats = (refs[part * count : (part + 1) * count] for part in range(3))
    so_far, (key_out, value_out) = refs[3 * count : -2], refs[-2:]
    blocks = key.shape[0] // BLOCK
    heads = key.shape[1] // HEAD_SIZE
    device = lax.axis_index("ctx")

    def one_head(head, _):
        part = columns_of(head)
        stat_at = pl.multiple_of(head * STAT_ROWS, STAT_ROWS)
        if so_far:
            key_out[:, part] = so_far[0][:, part]
            value_out[:, part] = so_far[1][:, part]
        for at, s in enumerate(sources):
            for i in range(blocks):
                rows = pl.ds(i * BLOCK, BLOCK)
                if s < 0:
                    place = rows
                else:
                    partner = jnp.bitwise_xor(device, 1 << s)
                    place = block_at(cols_ref[s, partner * blocks + i] - device * blocks)
                q, g = queries[at][rows, part], grads[at][rows, part]
                stat = stats[at][pl.ds(stat_at, STAT_ROWS), rows]
                top, scale, delta = stat[0:1], stat[1:2], stat[2:3]
                weights = jnp.exp(dot(key[place, part], q, NT) * FACTOR - top) * scale
                prob_grad = dot(value[place, part], g, NT)
                score_grad = (weights * (prob_grad - delta)).astype(BF16)
                key_term = dot(score_grad, q)
                value_term = dot(weights.astype(BF16), g)
                if s < 0:
                    key_out[place, part] = key_term
                    value_out[place, part] = value_term
                else:
                    key_out[place, part] += key_term
                    value_out[place, part] += value_term

    lax.fori_loop(0, heads, one_head, None)


def key_side(sources, cols, key, value, queries, grads, stats, so_far=()):
    shape = like(key.shape, F32)
    return call(
        functools.partial(key_kernel, sources),
        [shape, shape],
        cols,
        key,
        value,
        *queries,
        *grads,
        *stats,
        *so_far,
        scalars=1,
    )


def final_kernel(scatter, key, value, kept, got, key_out, value_out):
    odd = jnp.bitwise_and(lax.axis_index("ctx"), 1) == 1
    kept_rows = dot(scatter[...], kept[...])
    got_rows = dot(scatter[...], got[...])
    key_rows = jnp.where(odd, got_rows, kept_rows)
    value_rows = jnp.where(odd, kept_rows, got_rows)
    key_out[...] = ((key[...] + key_rows) * FACTOR).astype(BF16)
    value_out[...] = (value[...] + value_rows).astype(BF16)


def finish(scatter, key, value, kept, got):
    shape = jax.ShapeDtypeStruct(key.shape, BF16)
    return call(final_kernel, [shape, shape], scatter, key, value, kept, got)


def per_device(query_act, key_act, value_act, out_weight, cotangent, butterfly_cols, global_cols):
    strides = butterfly_cols.shape[1]
    groups = lax.axis_size("head")
    cube = strides == 3 and lax.axis_size("ctx") == 1 << strides
    cols = butterfly_cols.T
    slots = global_cols.shape[0]
    rows, width = key_act.shape
    masks = [1 << s for s in range(strides)]
    held = (0, *masks) if cube else (0,)
    owners = ((3, 5), (6, 7)) if cube else ()

    scatter, *hot = call(
        functools.partial(hot_kernel, held, owners),
        [like((rows, slots))]
        + [like((slots, rows))] * len(held)
        + [like((slots, HEAD_SIZE), F32)] * len(owners),
        global_cols.reshape(1, -1),
    )
    selects, owned = hot[: len(held)], hot[len(held) :]
    near_keys = [key_act] + [swap(key_act, "ctx", m) for m in masks]
    near_values = [value_act] + [swap(value_act, "ctx", m) for m in masks]
    pieces = [cotangent] + [swap(cotangent, "head", m) for m in range(1, groups)]
    far_query = [swap(query_act, "ctx", m) for m in masks]
    if cube:
        glob = []
        for near in (near_keys, near_values):
            have = select_globals(selects, near)
            have = merge(have, swap(have, "ctx", 1), owned[0])
            glob.append([have, swap(have, "ctx", 2)])
        glob_keys, glob_values = glob
    else:
        parts = (select_globals(selects, [key_act]), select_globals(selects, [value_act]))
        glob_keys, glob_values = ([part] for part in lax.psum(parts, "ctx"))
    attn_grad = call(grad_kernel, [like((rows, width))], out_weight, *pieces)[0]
    far_grad = [swap(attn_grad, "ctx", m) for m in masks]
    attention, query_grad, keep, send, stats = query_side(
        cols,
        query_act,
        attn_grad,
        key_act,
        value_act,
        near_keys[1:],
        near_values[1:],
        glob_keys,
        glob_values,
        owned[1:],
    )
    far_stats = [swap(stats, "ctx", m) for m in masks]
    if cube:
        total = keep + swap(send, "ctx", 1).astype(F32)
        total = total + swap(total.astype(BF16), "ctx", 2).astype(F32)
        total = total + swap(total.astype(BF16), "ctx", 6).astype(F32)
        kept = total.astype(BF16)
        got = swap(kept, "ctx", 1)
    else:
        odd = jnp.bitwise_and(lax.axis_index("ctx"), 1) == 1
        send = send.astype(F32)
        key_term, value_term = lax.psum(
            (jnp.where(odd, send, keep), jnp.where(odd, keep, send)), "ctx"
        )
        kept = jnp.where(odd, value_term, key_term).astype(BF16)
        got = jnp.where(odd, key_term, value_term).astype(BF16)
    term = out_weight.shape[1] // groups
    shapes = [like((rows, term), F32 if m == 0 else BF16) for m in range(groups)]
    terms = call(project_kernel, shapes, attention, out_weight)
    layer_out = terms[0]
    for m in range(1, groups):
        layer_out = layer_out + swap(terms[m], "head", m).astype(F32)
    so_far = key_side((-1,), cols, key_act, value_act, [query_act], [attn_grad], [stats])
    key_sum, value_sum = key_side(
        tuple(range(strides)), cols, key_act, value_act, far_query, far_grad, far_stats, so_far
    )
    key_grad, value_grad = finish(scatter, key_sum, value_sum, kept, got)
    return (layer_out.astype(BF16), query_grad, key_grad, value_grad)


def solution(mesh):
    in_specs = (
        P("ctx", "head"),
        P("ctx", "head"),
        P("ctx", "head"),
        P("head", None),
        P("ctx", "head"),
        P(),
        P(),
    )
    out_specs = (P("ctx", "head"),) * 4

    return jax.shard_map(
        per_device, mesh=mesh, in_specs=in_specs, out_specs=out_specs, check_vma=False
    )
```

```python
import functools
import math

import jax
import jax.numpy as jnp
from jax import lax
from jax.experimental import pallas as pl
from jax.experimental.pallas import tpu as pltpu
from jax.sharding import PartitionSpec as P


HEAD_SIZE = 128
BLOCK = 128
STAT_ROWS = 8
KERNEL_VMEM = 16 * 2**20


FACTOR = 1.0 / math.sqrt(HEAD_SIZE)
NT = (((1,), (1,)), ((), ()))
TN = (((0,), (0,)), ((), ()))
F32 = jnp.float32
BF16 = jnp.bfloat16


def swap(shard, axis, mask):
    return lax.ppermute(shard, axis, [(i, i ^ mask) for i in range(lax.axis_size(axis))])


def call(kernel, out_shape, *operands, scalars=0, scratch=()):
    in_specs = [pl.BlockSpec(memory_space=pltpu.SMEM)] * scalars
    in_specs += [pl.BlockSpec(memory_space=pltpu.VMEM)] * (len(operands) - scalars)
    outs = [pl.BlockSpec(memory_space=pltpu.VMEM)] * len(out_shape)
    placed = [pltpu.with_memory_space_constraint(o, pltpu.VMEM) for o in operands[scalars:]]
    return pl.pallas_call(
        kernel,
        in_specs=in_specs,
        out_specs=outs,
        out_shape=out_shape,
        scratch_shapes=scratch,
        compiler_params=pltpu.CompilerParams(vmem_limit_bytes=KERNEL_VMEM),
    )(*operands[:scalars], *placed)


def like(shape, dtype=jnp.bfloat16):
    return pltpu.VMEM(shape, dtype)


def dot(a, b, dims=(((1,), (0,)), ((), ()))):
    return lax.dot_general(a, b, dims, preferred_element_type=F32)


def block_at(index):
    return pl.ds(pl.multiple_of(index * BLOCK, BLOCK), BLOCK)


def columns_of(head):
    return pl.ds(pl.multiple_of(head * HEAD_SIZE, HEAD_SIZE), HEAD_SIZE)


def grad_kernel(weight_ref, *refs):
    pieces, out_ref = refs[:-1], refs[-1]
    width = pieces[0].shape[1]
    mine = lax.axis_index("head")
    total = None
    for m, piece in enumerate(pieces):
        start = pl.multiple_of(jnp.bitwise_xor(mine, m) * width, width)
        part = dot(piece[...], weight_ref[:, pl.ds(start, width)], NT)
        total = part if total is None else total + part
    out_ref[...] = total.astype(BF16)


def project_kernel(att_ref, weight_ref, *outs):
    width = outs[0].shape[1]
    mine = lax.axis_index("head")
    for m, out in enumerate(outs):
        start = pl.multiple_of(jnp.bitwise_xor(mine, m) * width, width)
        out[...] = dot(att_ref[...], weight_ref[:, pl.ds(start, width)]).astype(out.dtype)


def hot_kernel(masks, groups, cols_ref, scatter_ref, *outs):
    rows, slots = scatter_ref.shape
    device = lax.axis_index("ctx")
    row_ids = lax.broadcasted_iota(jnp.int32, (rows, slots), 0)

    def local(mask):
        return cols_ref[...] - jnp.bitwise_xor(device, mask) * rows

    for mask, out in zip(masks, outs):
        chosen = (row_ids == local(mask)).astype(F32)
        if mask == 0:
            scatter_ref[...] = chosen.astype(BF16)
        out[...] = chosen.T.astype(BF16)
    for group, out in zip(groups, outs[len(masks) :]):
        owned = 0.0
        for mask in group:
            at = jnp.broadcast_to(local(mask), (out.shape[1], slots))
            owned = owned + jnp.logical_and(at >= 0, at < rows).astype(F32)
        out[...] = owned.T


def select_kernel(count, *refs):
    total = dot(refs[0][...], refs[count][...])
    for select, source in zip(refs[1:count], refs[count + 1 : -1]):
        total = total + dot(select[...], source[...])
    refs[-1][...] = total.astype(BF16)


def select_globals(selects, sources):
    shape = like((selects[0].shape[0], sources[0].shape[1]))
    kernel = functools.partial(select_kernel, len(selects))
    return call(kernel, [shape], *selects, *sources)[0]


def merged(parts, owned, at):
    total = parts[0][:, at].astype(F32)
    for part, mask in zip(parts[1:], owned):
        total = total + mask[...] * part[:, at].astype(F32)
    return total.astype(BF16)


def merge_kernel(have, got, owned, out):
    for start in range(0, out.shape[1], HEAD_SIZE):
        part = pl.ds(start, HEAD_SIZE)
        out[:, part] = merged((have, got), (owned,), part)


def merge(have, got, owned):
    return call(merge_kernel, [like(have.shape)], have, got, owned)[0]


def near_at(strides, device, blocks, i, cols_ref, own, far, part):
    picked = [
        far[s][
            block_at(cols_ref[s, device * blocks + i] - jnp.bitwise_xor(device, 1 << s) * blocks),
            part,
        ]
        for s in range(strides)
    ]
    return jnp.concatenate([own[pl.ds(i * BLOCK, BLOCK), part]] + picked, 0)


def put_columns(ref, rows, head, columns):
    held = ref[rows, :]
    lane = lax.broadcasted_iota(jnp.int32, held.shape, 1)
    for place, column in enumerate(columns):
        held = jnp.where(lane == head * STAT_ROWS + place, column, held)
    ref[rows, :] = held


def take_column(ref, rows, head, place):
    held = ref[rows, :]
    lane = lax.broadcasted_iota(jnp.int32, held.shape, 1)
    return jnp.sum(jnp.where(lane == head * STAT_ROWS + place, held, 0.0), axis=1, keepdims=True)


def near_kernel(strides, cols_ref, query, grad, *refs):
    own_key, own_value = refs[:2]
    far_keys, far_values = refs[2 : 2 + strides], refs[2 + strides : 2 + 2 * strides]
    exponent_out, prob_out, stats = refs[-3:]
    blocks, heads = query.shape[0] // BLOCK, query.shape[1] // HEAD_SIZE
    near = (strides + 1) * BLOCK
    device = lax.axis_index("ctx")

    def one_head(head, _):
        part = columns_of(head)
        wide = pl.ds(pl.multiple_of(head * near, near), near)
        for i in range(blocks):
            rows = pl.ds(i * BLOCK, BLOCK)
            keys = near_at(strides, device, blocks, i, cols_ref, own_key, far_keys, part)
            values = near_at(strides, device, blocks, i, cols_ref, own_value, far_values, part)
            scores = dot(query[rows, part], keys, NT) * FACTOR
            top = jnp.max(scores, axis=1, keepdims=True)
            exponent = jnp.exp(scores - top)
            prob_grad = dot(grad[rows, part], values, NT)
            exponent_out[rows, wide] = exponent
            prob_out[rows, wide] = prob_grad
            total = jnp.sum(exponent, axis=1, keepdims=True)
            weighted = jnp.sum(exponent * prob_grad, axis=1, keepdims=True)
            put_columns(stats, rows, head, (top, total, weighted))

    lax.fori_loop(0, heads, one_head, None, unroll=2)


def glob_kernel(key_parts, value_parts, query, grad, near_stats, *refs):
    keys_in, refs = refs[:key_parts], refs[key_parts:]
    values_in, refs = refs[:value_parts], refs[value_parts:]
    key_masks, refs = refs[: key_parts - 1], refs[key_parts - 1 :]
    value_masks, refs = refs[: value_parts - 1], refs[value_parts - 1 :]
    keep_out, send_out, stat_out, rest_out, weight_out, score_out, key_out, value_out, stats = refs
    heads, slots = query.shape[1] // HEAD_SIZE, keep_out.shape[0]
    odd = jnp.bitwise_and(lax.axis_index("ctx"), 1) == 1
    every = pl.ds(0, query.shape[0])

    def one_head(head, _):
        part = columns_of(head)
        wide = pl.ds(pl.multiple_of(head * slots, slots), slots)
        keys = merged(keys_in, key_masks, part)
        values = merged(values_in, value_masks, part)
        key_out[:, part] = keys
        value_out[:, part] = values
        near_top, near_total, near_weighted = (
            take_column(near_stats, every, head, place) for place in range(3)
        )
        scores = dot(query[:, part], keys, NT) * FACTOR
        prob_grad = dot(grad[:, part], values, NT)
        top = jnp.maximum(near_top, jnp.max(scores, axis=1, keepdims=True))
        exponent = jnp.exp(scores - top)
        shrink = jnp.exp(near_top - top)
        scale = 1.0 / (shrink * near_total + jnp.sum(exponent, axis=1, keepdims=True))
        weights = exponent * scale
        near_scale = shrink * scale
        delta = near_scale * near_weighted + jnp.sum(weights * prob_grad, axis=1, keepdims=True)
        score_grad = (weights * (prob_grad - delta)).astype(BF16)
        rounded = weights.astype(BF16)
        weight_out[:, wide] = rounded
        score_out[:, wide] = score_grad
        key_term = dot(score_grad, query[:, part], TN)
        value_term = dot(rounded, grad[:, part], TN)
        keep_out[:, part] = jnp.where(odd, value_term, key_term)
        send_out[:, part] = jnp.where(odd, key_term, value_term).astype(BF16)
        put_columns(stats, every, head, (top, scale, delta))
        put_columns(rest_out, every, head, (near_scale, delta))

    lax.fori_loop(0, heads, one_head, None, unroll=2)
    for start in range(0, query.shape[0], BLOCK):
        rows = pl.ds(start, BLOCK)
        stat_out[:, rows] = stats[rows, :].T[: stat_out.shape[0]]


def rest_kernel(strides, cols_ref, exponents, probs, rest, weights_in, scores_in, *refs):
    glob_key, glob_value, own_key, own_value = refs[:4]
    far_keys, far_values = refs[4 : 4 + strides], refs[4 + strides : 4 + 2 * strides]
    att_out, query_out = refs[-2:]
    blocks, heads = own_key.shape[0] // BLOCK, own_key.shape[1] // HEAD_SIZE
    near, slots = (strides + 1) * BLOCK, glob_key.shape[0]
    device = lax.axis_index("ctx")

    def one_head(head, _):
        part = columns_of(head)
        wide = pl.ds(pl.multiple_of(head * near, near), near)
        glob = pl.ds(pl.multiple_of(head * slots, slots), slots)
        for i in range(blocks):
            rows = pl.ds(i * BLOCK, BLOCK)
            keys = near_at(strides, device, blocks, i, cols_ref, own_key, far_keys, part)
            values = near_at(strides, device, blocks, i, cols_ref, own_value, far_values, part)
            near_scale, delta = (take_column(rest, rows, head, place) for place in range(2))
            weights = exponents[rows, wide] * near_scale
            score_grad = (weights * (probs[rows, wide] - delta)).astype(BF16)
            attention = dot(weights.astype(BF16), values)
            attention = attention + dot(weights_in[rows, glob], glob_value[:, part])
            att_out[rows, part] = attention.astype(BF16)
            query_sum = dot(score_grad, keys) + dot(scores_in[rows, glob], glob_key[:, part])
            query_out[rows, part] = (query_sum * FACTOR).astype(BF16)

    lax.fori_loop(0, heads, one_head, None, unroll=2)


def key_kernel(sources, cols_ref, key, value, *refs):
    count = len(sources)
    queries, grads, stats = (refs[part * count : (part + 1) * count] for part in range(3))
    so_far, (key_out, value_out) = refs[3 * count : -2], refs[-2:]
    blocks = key.shape[0] // BLOCK
    heads = key.shape[1] // HEAD_SIZE
    device = lax.axis_index("ctx")

    def one_head(head, _):
        part = columns_of(head)
        stat_at = pl.multiple_of(head * STAT_ROWS, STAT_ROWS)
        if so_far:
            key_out[:, part] = so_far[0][:, part]
            value_out[:, part] = so_far[1][:, part]
        for at, s in enumerate(sources):
            for i in range(blocks):
                rows = pl.ds(i * BLOCK, BLOCK)
                if s < 0:
                    place = rows
                else:
                    partner = jnp.bitwise_xor(device, 1 << s)
                    place = block_at(cols_ref[s, partner * blocks + i] - device * blocks)
                q, g = queries[at][rows, part], grads[at][rows, part]
                stat = stats[at][pl.ds(stat_at, STAT_ROWS), rows]
                top, scale, delta = stat[0:1], stat[1:2], stat[2:3]
                weights = jnp.exp(dot(key[place, part], q, NT) * FACTOR - top) * scale
                prob_grad = dot(value[place, part], g, NT)
                score_grad = (weights * (prob_grad - delta)).astype(BF16)
                key_term = dot(score_grad, q)
                value_term = dot(weights.astype(BF16), g)
                if s < 0:
                    key_out[place, part] = key_term
                    value_out[place, part] = value_term
                else:
                    key_out[place, part] += key_term
                    value_out[place, part] += value_term

    lax.fori_loop(0, heads, one_head, None)


def key_side(sources, cols, key, value, queries, grads, stats, so_far=()):
    shape = like(key.shape, F32)
    return call(
        functools.partial(key_kernel, sources),
        [shape, shape],
        cols,
        key,
        value,
        *queries,
        *grads,
        *stats,
        *so_far,
        scalars=1,
    )


def final_kernel(scatter, key, value, kept, got, key_out, value_out):
    odd = jnp.bitwise_and(lax.axis_index("ctx"), 1) == 1
    kept_rows = dot(scatter[...], kept[...])
    got_rows = dot(scatter[...], got[...])
    key_rows = jnp.where(odd, got_rows, kept_rows)
    value_rows = jnp.where(odd, kept_rows, got_rows)
    key_out[...] = ((key[...] + key_rows) * FACTOR).astype(BF16)
    value_out[...] = (value[...] + value_rows).astype(BF16)


def finish(scatter, key, value, kept, got):
    shape = jax.ShapeDtypeStruct(key.shape, BF16)
    return call(final_kernel, [shape, shape], scatter, key, value, kept, got)


def per_device(query_act, key_act, value_act, out_weight, cotangent, butterfly_cols, global_cols):
    strides = butterfly_cols.shape[1]
    groups = lax.axis_size("head")
    cube = strides == 3 and lax.axis_size("ctx") == 1 << strides
    cols = butterfly_cols.T
    slots = global_cols.shape[0]
    rows, width = key_act.shape
    masks = [1 << s for s in range(strides)]
    held = (0, *masks) if cube else (0,)
    owners = ((3, 5), (6, 7), (6,), (7,)) if cube else ()

    scatter, *hot = call(
        functools.partial(hot_kernel, held, owners),
        [like((rows, slots))]
        + [like((slots, rows))] * len(held)
        + [like((slots, HEAD_SIZE), F32)] * len(owners),
        global_cols.reshape(1, -1),
    )
    selects, owned = hot[: len(held)], hot[len(held) :]
    near_keys = [key_act] + [swap(key_act, "ctx", m) for m in masks]
    near_values = [value_act] + [swap(value_act, "ctx", m) for m in masks]
    pieces = [cotangent] + [swap(cotangent, "head", m) for m in range(1, groups)]
    far_query = [swap(query_act, "ctx", m) for m in masks]
    key_masks, value_masks = [], []
    if cube:
        have = select_globals(selects, near_keys)
        have = merge(have, swap(have, "ctx", 1), owned[0])
        glob_keys, key_masks = [have, swap(have, "ctx", 2)], owned[1:2]
        have = select_globals(selects, near_values)
        glob_values = [have] + [swap(have, "ctx", m) for m in (1, 2, 3)]
        value_masks = [owned[0], owned[2], owned[3]]
    else:
        parts = (select_globals(selects, [key_act]), select_globals(selects, [value_act]))
        glob_keys, glob_values = ([part] for part in lax.psum(parts, "ctx"))
    attn_grad = call(grad_kernel, [like((rows, width))], out_weight, *pieces)[0]
    far_grad = [swap(attn_grad, "ctx", m) for m in masks]
    near_all = [key_act, value_act, *near_keys[1:], *near_values[1:]]
    heads = width // HEAD_SIZE
    near = (strides + 1) * BLOCK
    exponents, probs, near_stats = call(
        functools.partial(near_kernel, strides),
        [like((rows, heads * near), F32)] * 2 + [like((rows, BLOCK), F32)],
        cols,
        query_act,
        attn_grad,
        *near_all,
        scalars=1,
    )
    keep, send, stats, rest, weights, scores, glob_key, glob_value = call(
        functools.partial(glob_kernel, len(glob_keys), len(glob_values)),
        [
            like((slots, width), F32),
            like((slots, width)),
            like((heads * STAT_ROWS, rows), F32),
            like((rows, BLOCK), F32),
            like((rows, heads * slots)),
            like((rows, heads * slots)),
            like((slots, width)),
            like((slots, width)),
        ],
        query_act,
        attn_grad,
        near_stats,
        *glob_keys,
        *glob_values,
        *key_masks,
        *value_masks,
        scratch=[pltpu.VMEM((rows, BLOCK), F32)],
    )
    attention, query_grad = call(
        functools.partial(rest_kernel, strides),
        [like((rows, width)), jax.ShapeDtypeStruct((rows, width), BF16)],
        cols,
        exponents,
        probs,
        rest,
        weights,
        scores,
        glob_key,
        glob_value,
        *near_all,
        scalars=1,
    )
    far_stats = [swap(stats, "ctx", m) for m in masks]
    if cube:
        total = keep + swap(send, "ctx", 1).astype(F32)
        total = total + swap(total.astype(BF16), "ctx", 2).astype(F32)
        total = total + swap(total.astype(BF16), "ctx", 6).astype(F32)
        kept = total.astype(BF16)
        got = swap(kept, "ctx", 1)
    else:
        odd = jnp.bitwise_and(lax.axis_index("ctx"), 1) == 1
        send = send.astype(F32)
        key_term, value_term = lax.psum(
            (jnp.where(odd, send, keep), jnp.where(odd, keep, send)), "ctx"
        )
        kept = jnp.where(odd, value_term, key_term).astype(BF16)
        got = jnp.where(odd, key_term, value_term).astype(BF16)
    term = out_weight.shape[1] // groups
    shapes = [like((rows, term), F32 if m == 0 else BF16) for m in range(groups)]
    terms = call(project_kernel, shapes, attention, out_weight)
    layer_out = terms[0]
    for m in range(1, groups):
        layer_out = layer_out + swap(terms[m], "head", m).astype(F32)
    so_far = key_side((-1,), cols, key_act, value_act, [query_act], [attn_grad], [stats])
    key_sum, value_sum = key_side(
        tuple(range(strides)), cols, key_act, value_act, far_query, far_grad, far_stats, so_far
    )
    key_grad, value_grad = finish(scatter, key_sum, value_sum, kept, got)
    return (layer_out.astype(BF16), query_grad, key_grad, value_grad)


def solution(mesh):
    in_specs = (
        P("ctx", "head"),
        P("ctx", "head"),
        P("ctx", "head"),
        P("head", None),
        P("ctx", "head"),
        P(),
        P(),
    )
    out_specs = (P("ctx", "head"),) * 4

    return jax.shard_map(
        per_device, mesh=mesh, in_specs=in_specs, out_specs=out_specs, check_vma=False
    )
```

```python
import functools
import math

import jax
import jax.numpy as jnp
from jax import lax
from jax.experimental import pallas as pl
from jax.experimental.pallas import tpu as pltpu
from jax.sharding import PartitionSpec as P


HEAD_SIZE = 128
BLOCK = 128
STAT_ROWS = 8
KERNEL_VMEM = 16 * 2**20


FACTOR = 1.0 / math.sqrt(HEAD_SIZE)
NT = (((1,), (1,)), ((), ()))
TN = (((0,), (0,)), ((), ()))
F32 = jnp.float32
BF16 = jnp.bfloat16


def swap(shard, axis, mask):
    return lax.ppermute(shard, axis, [(i, i ^ mask) for i in range(lax.axis_size(axis))])


def call(kernel, out_shape, *operands, scalars=0, scratch=()):
    in_specs = [pl.BlockSpec(memory_space=pltpu.SMEM)] * scalars
    in_specs += [pl.BlockSpec(memory_space=pltpu.VMEM)] * (len(operands) - scalars)
    outs = [pl.BlockSpec(memory_space=pltpu.VMEM)] * len(out_shape)
    placed = [pltpu.with_memory_space_constraint(o, pltpu.VMEM) for o in operands[scalars:]]
    return pl.pallas_call(
        kernel,
        in_specs=in_specs,
        out_specs=outs,
        out_shape=out_shape,
        scratch_shapes=scratch,
        compiler_params=pltpu.CompilerParams(vmem_limit_bytes=KERNEL_VMEM),
    )(*operands[:scalars], *placed)


def like(shape, dtype=jnp.bfloat16):
    return pltpu.VMEM(shape, dtype)


def dot(a, b, dims=(((1,), (0,)), ((), ()))):
    return lax.dot_general(a, b, dims, preferred_element_type=F32)


def block_at(index):
    return pl.ds(pl.multiple_of(index * BLOCK, BLOCK), BLOCK)


def columns_of(head):
    return pl.ds(pl.multiple_of(head * HEAD_SIZE, HEAD_SIZE), HEAD_SIZE)


def grad_kernel(weight_ref, query, *refs):
    pieces, (out_ref, pair_ref) = refs[:-2], refs[-2:]
    rows = query.shape[0]
    width = pieces[0].shape[1]
    mine = lax.axis_index("head")
    total = None
    for m, piece in enumerate(pieces):
        start = pl.multiple_of(jnp.bitwise_xor(mine, m) * width, width)
        part = dot(piece[...], weight_ref[:, pl.ds(start, width)], NT)
        total = part if total is None else total + part
    out_ref[...] = total.astype(BF16)
    pair_ref[:rows, :] = query[...]
    pair_ref[rows:, :] = total.astype(BF16)


def project_kernel(att_ref, weight_ref, *outs):
    width = outs[0].shape[1]
    mine = lax.axis_index("head")
    for m, out in enumerate(outs):
        start = pl.multiple_of(jnp.bitwise_xor(mine, m) * width, width)
        out[...] = dot(att_ref[...], weight_ref[:, pl.ds(start, width)]).astype(out.dtype)


def hot_kernel(masks, groups, cols_ref, scatter_ref, *outs):
    rows, slots = scatter_ref.shape
    device = lax.axis_index("ctx")
    row_ids = lax.broadcasted_iota(jnp.int32, (rows, slots), 0)

    def local(mask):
        return cols_ref[...] - jnp.bitwise_xor(device, mask) * rows

    for mask, out in zip(masks, outs):
        chosen = (row_ids == local(mask)).astype(F32)
        if mask == 0:
            scatter_ref[...] = chosen.astype(BF16)
        out[...] = chosen.T.astype(BF16)
    for group, out in zip(groups, outs[len(masks) :]):
        owned = 0.0
        for mask in group:
            at = jnp.broadcast_to(local(mask), (out.shape[1], slots))
            owned = owned + jnp.logical_and(at >= 0, at < rows).astype(F32)
        out[...] = owned.T


def select_kernel(count, *refs):
    total = dot(refs[0][...], refs[count][...])
    for select, source in zip(refs[1:count], refs[count + 1 : -1]):
        total = total + dot(select[...], source[...])
    refs[-1][...] = total.astype(BF16)


def select_globals(selects, sources):
    shape = like((selects[0].shape[0], sources[0].shape[1]))
    kernel = functools.partial(select_kernel, len(selects))
    return call(kernel, [shape], *selects, *sources)[0]


def merged(parts, owned, at):
    total = parts[0][:, at].astype(F32)
    for part, mask in zip(parts[1:], owned):
        total = total + mask[...] * part[:, at].astype(F32)
    return total.astype(BF16)


def merge_kernel(have, got, owned, out):
    for start in range(0, out.shape[1], HEAD_SIZE):
        part = pl.ds(start, HEAD_SIZE)
        out[:, part] = merged((have, got), (owned,), part)


def merge(have, got, owned):
    return call(merge_kernel, [like(have.shape)], have, got, owned)[0]


def near_at(strides, device, blocks, i, cols_ref, own, far, part):
    picked = [
        far[s][
            block_at(cols_ref[s, device * blocks + i] - jnp.bitwise_xor(device, 1 << s) * blocks),
            part,
        ]
        for s in range(strides)
    ]
    return jnp.concatenate([own[pl.ds(i * BLOCK, BLOCK), part]] + picked, 0)


def put_columns(ref, rows, head, columns, step=1, width=STAT_ROWS):
    held = ref[rows, :]
    lane = lax.broadcasted_iota(jnp.int32, held.shape, 1)
    for place, column in enumerate(columns):
        held = jnp.where(lane == head * width + place * step, column, held)
    ref[rows, :] = held


def take_column(ref, rows, head, place):
    held = ref[rows, :]
    lane = lax.broadcasted_iota(jnp.int32, held.shape, 1)
    return jnp.sum(jnp.where(lane == head * STAT_ROWS + place, held, 0.0), axis=1, keepdims=True)


NOTES = 7


def thirds(column):
    high = column.astype(BF16).astype(F32)
    middle = (column - high).astype(BF16).astype(F32)
    return high, middle, column - high - middle


def note_lines(rows, width):
    groups = width // rows
    lines = -(-NOTES * (width // HEAD_SIZE) // groups)
    return groups, -(-lines // 16) * 16


def read_notes(message, stats, rows, heads):
    _, lines = note_lines(rows, message.shape[1])
    held = message[message.shape[0] - lines :, :].astype(F32)

    def line(place, head):
        group, at = divmod(place * heads + head, lines)
        return held[at : at + 1, group * rows : (group + 1) * rows]

    for head in range(heads):
        for place, parts in enumerate(((0,), (1, 2, 3), (4, 5, 6))):
            at = head * STAT_ROWS + place
            stats[at : at + 1, :] = sum(line(part, head) for part in parts)


def near_kernel(strides, parts, cols_ref, query, grad, *refs):
    own_key, own_value = refs[:2]
    far_keys, far_values = refs[2 : 2 + strides], refs[2 + strides : 2 + 2 * strides]
    globs, owned = refs[2 + 2 * strides :][:parts], refs[2 + 2 * strides + parts : -6]
    weight_out, prob_out, glob_out, term_out, key_out, stats = refs[-6:]
    blocks, heads = query.shape[0] // BLOCK, query.shape[1] // HEAD_SIZE
    near, slots = (strides + 1) * BLOCK, key_out.shape[0]
    device = lax.axis_index("ctx")

    def one_head(head, _):
        part = columns_of(head)
        wide = pl.ds(pl.multiple_of(head * near, near), near)
        glob = pl.ds(pl.multiple_of(head * slots, slots), slots)
        glob_key = merged(globs, owned, part)
        key_out[:, part] = glob_key
        rounded = []
        for i in range(blocks):
            rows = pl.ds(i * BLOCK, BLOCK)
            keys = near_at(strides, device, blocks, i, cols_ref, own_key, far_keys, part)
            values = near_at(strides, device, blocks, i, cols_ref, own_value, far_values, part)
            scores = dot(query[rows, part], jnp.concatenate([keys, glob_key], 0), NT) * FACTOR
            prob_grad = dot(grad[rows, part], values, NT)
            top = jnp.max(scores, axis=1, keepdims=True)
            top = top.astype(BF16).astype(F32)
            exponent = jnp.exp(scores - top)
            scale = 1.0 / jnp.sum(exponent, axis=1, keepdims=True)
            weights = exponent * scale
            weight_out[rows, wide] = weights[:, :near]
            prob_out[rows, wide] = prob_grad
            glob_out[rows, glob] = weights[:, near:]
            rounded.append(weights[:, near:].astype(BF16))
            delta = jnp.sum(weights[:, :near] * prob_grad, axis=1, keepdims=True)
            put_columns(stats, rows, head, (top, scale, delta))
        term_out[:, part] = dot(jnp.concatenate(rounded, 0), grad[:, part], TN)

    lax.fori_loop(0, heads, one_head, None, unroll=2)


def glob_kernel(parts, query, grad, near_stats, weights_in, value_term, *refs):
    values_in, owned = refs[:parts], refs[parts : 2 * parts - 1]
    keep_out, send_out, delta_out, score_out, value_out, stats = refs[2 * parts - 1 :]
    heads, slots = query.shape[1] // HEAD_SIZE, value_out.shape[0]
    odd = jnp.bitwise_and(lax.axis_index("ctx"), 1) == 1
    every = pl.ds(0, query.shape[0])

    def one_head(head, _):
        part = columns_of(head)
        glob = pl.ds(pl.multiple_of(head * slots, slots), slots)
        values = merged(values_in, owned, part)
        value_out[:, part] = values
        prob_grad = dot(grad[:, part], values, NT)
        top, scale, near_delta = (take_column(near_stats, every, head, place) for place in range(3))
        weights = weights_in[:, glob]
        delta = near_delta + jnp.sum(weights * prob_grad, axis=1, keepdims=True)
        score_grad = (weights * (prob_grad - delta)).astype(BF16)
        score_out[:, glob] = score_grad
        key_term = dot(score_grad, query[:, part], TN)
        keep_out[:, part] = jnp.where(odd, value_term[:, part], key_term)
        send_out[:slots, part] = jnp.where(odd, key_term, value_term[:, part]).astype(BF16)
        notes = (top, *thirds(scale), *thirds(delta))
        put_columns(stats, every, head, notes, step=heads, width=1)
        put_columns(delta_out, every, head, (delta,))

    lax.fori_loop(0, heads, one_head, None, unroll=2)
    groups, lines = note_lines(query.shape[0], query.shape[1])
    for start in range(0, query.shape[0], BLOCK):
        turned = stats[pl.ds(start, BLOCK), :].T
        for group in range(groups):
            at = pl.ds(group * query.shape[0] + start, BLOCK)
            send_out[slots:, at] = turned[group * lines : (group + 1) * lines].astype(BF16)


def rest_kernel(strides, cols_ref, weights_in, probs, deltas, glob_weights, scores_in, *refs):
    glob_key, glob_value, own_key, own_value = refs[:4]
    far_keys, far_values = refs[4 : 4 + strides], refs[4 + strides : 4 + 2 * strides]
    att_out, query_out = refs[-2:]
    blocks, heads = own_key.shape[0] // BLOCK, own_key.shape[1] // HEAD_SIZE
    near, slots = (strides + 1) * BLOCK, glob_key.shape[0]
    device = lax.axis_index("ctx")

    def one_head(head, _):
        part = columns_of(head)
        wide = pl.ds(pl.multiple_of(head * near, near), near)
        glob = pl.ds(pl.multiple_of(head * slots, slots), slots)
        for i in range(blocks):
            rows = pl.ds(i * BLOCK, BLOCK)
            keys = near_at(strides, device, blocks, i, cols_ref, own_key, far_keys, part)
            values = near_at(strides, device, blocks, i, cols_ref, own_value, far_values, part)
            delta = take_column(deltas, rows, head, 0)
            weights = weights_in[rows, wide]
            score_grad = (weights * (probs[rows, wide] - delta)).astype(BF16)
            attention = dot(weights.astype(BF16), values)
            attention = attention + dot(glob_weights[rows, glob].astype(BF16), glob_value[:, part])
            att_out[rows, part] = attention.astype(BF16)
            query_sum = dot(score_grad, keys) + dot(scores_in[rows, glob], glob_key[:, part])
            query_out[rows, part] = (query_sum * FACTOR).astype(BF16)

    lax.fori_loop(0, heads, one_head, None, unroll=2)


def key_kernel(s, count, cols_ref, key, value, *refs):
    *pair, message = refs[: count + 1]
    so_far, (key_out, value_out, stats) = refs[count + 1 : -3], refs[-3:]
    blocks = key.shape[0] // BLOCK
    heads = key.shape[1] // HEAD_SIZE
    device = lax.axis_index("ctx")
    read_notes(message, stats, key.shape[0], heads)
    grad_start = 0 if count > 1 else pair[0].shape[0] // 2

    def one_head(head, _):
        part = columns_of(head)
        stat_at = pl.multiple_of(head * STAT_ROWS, STAT_ROWS)
        if so_far:
            key_out[:, part] = so_far[0][:, part]
            value_out[:, part] = so_far[1][:, part]
        for i in range(blocks):
            rows = pl.ds(i * BLOCK, BLOCK)
            if s < 0:
                place = rows
            else:
                partner = jnp.bitwise_xor(device, 1 << s)
                place = block_at(cols_ref[s, partner * blocks + i] - device * blocks)
            q = pair[0][rows, part]
            g = pair[-1][pl.ds(grad_start + i * BLOCK, BLOCK), part]
            stat = stats[pl.ds(stat_at, STAT_ROWS), rows]
            top, scale, delta = stat[0:1], stat[1:2], stat[2:3]
            weights = jnp.exp(dot(key[place, part], q, NT) * FACTOR - top) * scale
            prob_grad = dot(value[place, part], g, NT)
            score_grad = (weights * (prob_grad - delta)).astype(BF16)
            key_term = dot(score_grad, q)
            value_term = dot(weights.astype(BF16), g)
            if s < 0:
                key_out[place, part] = key_term
                value_out[place, part] = value_term
            else:
                key_out[place, part] += key_term
                value_out[place, part] += value_term

    lax.fori_loop(0, heads, one_head, None)


def key_side(source, cols, key, value, pair, message, so_far=()):
    shape = like(key.shape, F32)
    heads = key.shape[1] // HEAD_SIZE
    return call(
        functools.partial(key_kernel, source, len(pair)),
        [shape, shape],
        cols,
        key,
        value,
        *pair,
        message,
        *so_far,
        scalars=1,
        scratch=[pltpu.VMEM((heads * STAT_ROWS, key.shape[0]), F32)],
    )


def bit_of(mask):
    return jnp.bitwise_and(lax.axis_index("ctx"), mask) != 0


def add_kernel(cut, last, total, got, mine, *outs):
    slots = total.shape[0]
    result = total[...] + got[:slots, :].astype(F32)
    send = result
    if cut:
        low, high, upper = result[: slots // 2], result[slots // 2 :], bit_of(cut)
        result, send = jnp.where(upper, high, low), jnp.where(upper, low, high)
    if last:
        outs[0][...] = result.astype(BF16)
    else:
        outs[0][...] = result
        outs[1][: send.shape[0], :] = send.astype(BF16)
        outs[1][send.shape[0] :, :] = mine[mine.shape[0] - outs[1].shape[0] + send.shape[0] :, :]


def add(total, got, mine, notes, cut=0, last=False):
    slots, width = total.shape
    slots = slots // 2 if cut else slots
    shapes = [like((slots, width))]
    if not last:
        shapes = [like((slots, width), F32), like((slots + notes, width))]
    return call(functools.partial(add_kernel, cut, last), shapes, total, got, mine)


def out_kernel(*refs):
    refs[-1][...] = sum((ref[...].astype(F32) for ref in refs[1:-1]), refs[0][...]).astype(BF16)


def final_kernel(cut, scatter, key, value, *refs):
    half = len(refs) // 2 - 1
    kept, got, (key_out, value_out) = refs[:half], refs[half:-2], refs[-2:]
    odd = bit_of(1)

    def rows_of(parts):
        if len(parts) == 1:
            return dot(scatter[...], parts[0][...])
        mine, other, upper = parts[0][...].astype(F32), parts[1][...].astype(F32), bit_of(cut)
        whole = [jnp.where(upper, other, mine), jnp.where(upper, mine, other)]
        return dot(scatter[...], jnp.concatenate(whole, 0).astype(BF16))

    kept_rows, got_rows = rows_of(kept), rows_of(got)
    key_rows = jnp.where(odd, got_rows, kept_rows)
    value_rows = jnp.where(odd, kept_rows, got_rows)
    key_out[...] = ((key[...] + key_rows) * FACTOR).astype(BF16)
    value_out[...] = (value[...] + value_rows).astype(BF16)


def finish(cut, scatter, key, value, kept, got):
    shape = jax.ShapeDtypeStruct(key.shape, BF16)
    kernel = functools.partial(final_kernel, cut)
    return call(kernel, [shape, shape], scatter, key, value, *kept, *got)


def per_device(query_act, key_act, value_act, out_weight, cotangent, butterfly_cols, global_cols):
    strides = butterfly_cols.shape[1]
    groups = lax.axis_size("head")
    cube = strides == 3 and lax.axis_size("ctx") == 1 << strides
    cols = butterfly_cols.T
    slots = global_cols.shape[0]
    rows, width = key_act.shape
    masks = [1 << s for s in range(strides)]
    held = (0, *masks) if cube else (0,)
    owners = ((3, 5), (6, 7)) if cube else ()

    scatter, *hot = call(
        functools.partial(hot_kernel, held, owners),
        [like((rows, slots))]
        + [like((slots, rows))] * len(held)
        + [like((slots, HEAD_SIZE), F32)] * len(owners),
        global_cols.reshape(1, -1),
    )
    selects, owned = hot[: len(held)], hot[len(held) :]
    near_keys = [key_act] + [swap(key_act, "ctx", m) for m in masks]
    near_values = [value_act] + [swap(value_act, "ctx", m) for m in masks]
    pieces = [cotangent] + [swap(cotangent, "head", m) for m in range(1, groups)]
    if cube:
        glob = []
        for near in (near_keys, near_values):
            have = select_globals(selects, near)
            have = merge(have, swap(have, "ctx", 1), owned[0])
            glob.append([have, swap(have, "ctx", 2)])
        glob_keys, glob_values = glob
    else:
        parts = (select_globals(selects, [key_act]), select_globals(selects, [value_act]))
        glob_keys, glob_values = ([part] for part in lax.psum(parts, "ctx"))
    attn_grad, pair = call(
        grad_kernel, [like((rows, width)), like((2 * rows, width))], out_weight, query_act, *pieces
    )
    pairs = [[pair]] + [[swap(pair, "ctx", m)] for m in masks[:-1]]
    m = masks[-1]
    pairs.append([swap(query_act, "ctx", m), swap(attn_grad, "ctx", m)])
    near_all = [key_act, value_act, *near_keys[1:], *near_values[1:]]
    heads = width // HEAD_SIZE
    near = (strides + 1) * BLOCK
    weights, probs, glob_weights, value_term, glob_key, near_stats = call(
        functools.partial(near_kernel, strides, len(glob_keys)),
        [
            like((rows, heads * near), F32),
            like((rows, heads * near), F32),
            like((rows, heads * slots), F32),
            like((slots, width), F32),
            like((slots, width)),
            like((rows, BLOCK), F32),
        ],
        cols,
        query_act,
        attn_grad,
        *near_all,
        *glob_keys,
        *owned[1:],
        scalars=1,
    )
    total, message, deltas, scores, glob_value = call(
        functools.partial(glob_kernel, len(glob_values)),
        [
            like((slots, width), F32),
            like((slots + note_lines(rows, width)[1], width)),
            like((rows, BLOCK), F32),
            like((rows, heads * slots)),
            like((slots, width)),
        ],
        query_act,
        attn_grad,
        near_stats,
        glob_weights,
        value_term,
        *glob_values,
        *owned[1:],
        scratch=[pltpu.VMEM((rows, BLOCK), F32)],
    )
    attention, query_grad = call(
        functools.partial(rest_kernel, strides),
        [like((rows, width)), jax.ShapeDtypeStruct((rows, width), BF16)],
        cols,
        weights,
        probs,
        deltas,
        glob_weights,
        scores,
        glob_key,
        glob_value,
        *near_all,
        scalars=1,
    )
    messages = [message]
    if cube:
        notes = note_lines(rows, width)[1]
        messages.append(swap(message, "ctx", 1))
        total, message = add(total, messages[1], messages[0], notes, cut=2)
        messages.append(swap(message, "ctx", 2))
        total, message = add(total, messages[2], messages[0], notes)
        messages.append(swap(message, "ctx", 4))
        (mine,) = add(total, messages[3], messages[0], notes, last=True)
        other = swap(mine, "ctx", 2)
        kept = [mine, other]
        got = [swap(mine, "ctx", 1), swap(other, "ctx", 1)]
    else:
        messages += [swap(message, "ctx", m) for m in masks]
        odd = jnp.bitwise_and(lax.axis_index("ctx"), 1) == 1
        send = message[:slots].astype(F32)
        key_term, value_term = lax.psum(
            (jnp.where(odd, send, total), jnp.where(odd, total, send)), "ctx"
        )
        kept = [jnp.where(odd, value_term, key_term).astype(BF16)]
        got = [jnp.where(odd, key_term, value_term).astype(BF16)]
    term = out_weight.shape[1] // groups
    shapes = [like((rows, term), F32 if m == 0 else BF16) for m in range(groups)]
    terms = call(project_kernel, shapes, attention, out_weight)
    parts = [swap(terms[m], "head", m) for m in range(1, groups)]
    out_shape = jax.ShapeDtypeStruct((rows, term), BF16)
    layer_out = call(out_kernel, [out_shape], terms[0], *parts)[0]
    so_far = ()
    for at, m in enumerate([0, *masks]):
        so_far = key_side(at - 1, cols, key_act, value_act, pairs[at], messages[at], so_far)
    key_sum, value_sum = so_far
    key_grad, value_grad = finish(2, scatter, key_sum, value_sum, kept, got)
    return (layer_out, query_grad, key_grad, value_grad)


def solution(mesh):
    in_specs = (
        P("ctx", "head"),
        P("ctx", "head"),
        P("ctx", "head"),
        P("head", None),
        P("ctx", "head"),
        P(),
        P(),
    )
    out_specs = (P("ctx", "head"),) * 4

    return jax.shard_map(
        per_device, mesh=mesh, in_specs=in_specs, out_specs=out_specs, check_vma=False
    )
```

```python
import functools
import math

import jax
import jax.numpy as jnp
from jax import lax
from jax.experimental import pallas as pl
from jax.experimental.pallas import tpu as pltpu
from jax.sharding import PartitionSpec as P


HEAD_SIZE = 128
BLOCK = 128
STAT_ROWS = 8
KERNEL_VMEM = 16 * 2**20


FACTOR = 1.0 / math.sqrt(HEAD_SIZE)
NT = (((1,), (1,)), ((), ()))
TN = (((0,), (0,)), ((), ()))
F32 = jnp.float32
BF16 = jnp.bfloat16


def swap(shard, axis, mask):
    return lax.ppermute(shard, axis, [(i, i ^ mask) for i in range(lax.axis_size(axis))])


def call(kernel, out_shape, *operands, scalars=0, scratch=(), outside=()):
    in_specs = [pl.BlockSpec(memory_space=pltpu.SMEM)] * scalars
    in_specs += [pl.BlockSpec(memory_space=pltpu.VMEM)] * (len(operands) - scalars + len(outside))
    outs = [pl.BlockSpec(memory_space=pltpu.VMEM)] * len(out_shape)
    placed = [pltpu.with_memory_space_constraint(o, pltpu.VMEM) for o in operands[scalars:]]
    return pl.pallas_call(
        kernel,
        in_specs=in_specs,
        out_specs=outs,
        out_shape=out_shape,
        scratch_shapes=scratch,
        compiler_params=pltpu.CompilerParams(vmem_limit_bytes=KERNEL_VMEM),
    )(*operands[:scalars], *placed, *outside)


def like(shape, dtype=jnp.bfloat16):
    return pltpu.VMEM(shape, dtype)


def dot(a, b, dims=(((1,), (0,)), ((), ()))):
    return lax.dot_general(a, b, dims, preferred_element_type=F32)


def block_at(index):
    return pl.ds(pl.multiple_of(index * BLOCK, BLOCK), BLOCK)


def columns_of(head):
    return pl.ds(pl.multiple_of(head * HEAD_SIZE, HEAD_SIZE), HEAD_SIZE)


def grad_kernel(weight_ref, query, *refs):
    pieces, (out_ref, pair_ref) = refs[:-2], refs[-2:]
    rows = query.shape[0]
    width = pieces[0].shape[1]
    mine = lax.axis_index("head")
    total = None
    for m, piece in enumerate(pieces):
        start = pl.multiple_of(jnp.bitwise_xor(mine, m) * width, width)
        part = dot(piece[...], weight_ref[:, pl.ds(start, width)], NT)
        total = part if total is None else total + part
    out_ref[...] = total.astype(BF16)
    pair_ref[:rows, :] = query[...]
    pair_ref[rows:, :] = total.astype(BF16)


def project_kernel(att_ref, weight_ref, *outs):
    width = outs[0].shape[1]
    mine = lax.axis_index("head")
    for m, out in enumerate(outs):
        start = pl.multiple_of(jnp.bitwise_xor(mine, m) * width, width)
        out[...] = dot(att_ref[...], weight_ref[:, pl.ds(start, width)]).astype(out.dtype)


def hot_kernel(masks, groups, cols_ref, key, value, key_copy, value_copy, scatter_ref, *outs):
    key_copy[...] = key[...]
    value_copy[...] = value[...]
    rows, slots = scatter_ref.shape
    device = lax.axis_index("ctx")
    row_ids = lax.broadcasted_iota(jnp.int32, (rows, slots), 0)

    def local(mask):
        return cols_ref[...] - jnp.bitwise_xor(device, mask) * rows

    for mask, out in zip(masks, outs):
        chosen = (row_ids == local(mask)).astype(F32)
        if mask == 0:
            scatter_ref[...] = chosen.astype(BF16)
        out[...] = chosen.T.astype(BF16)
    for group, out in zip(groups, outs[len(masks) :]):
        owned = 0.0
        for mask in group:
            at = jnp.broadcast_to(local(mask), (out.shape[1], slots))
            owned = owned + jnp.logical_and(at >= 0, at < rows).astype(F32)
        out[...] = owned.T


def select_kernel(count, *refs):
    total = dot(refs[0][...], refs[count][...])
    for select, source in zip(refs[1:count], refs[count + 1 : -1]):
        total = total + dot(select[...], source[...])
    refs[-1][...] = total.astype(BF16)


def select_globals(selects, sources):
    shape = like((selects[0].shape[0], sources[0].shape[1]))
    kernel = functools.partial(select_kernel, len(selects))
    return call(kernel, [shape], *selects, *sources)[0]


def merged(parts, owned, at):
    total = parts[0][:, at].astype(F32)
    for part, mask in zip(parts[1:], owned):
        total = total + mask[...] * part[:, at].astype(F32)
    return total.astype(BF16)


def merge_kernel(have, got, owned, out):
    for start in range(0, out.shape[1], HEAD_SIZE):
        part = pl.ds(start, HEAD_SIZE)
        out[:, part] = merged((have, got), (owned,), part)


def merge(have, got, owned):
    return call(merge_kernel, [like(have.shape)], have, got, owned)[0]


def near_at(strides, device, blocks, i, cols_ref, own, far, part):
    picked = [
        far[s][
            block_at(cols_ref[s, device * blocks + i] - jnp.bitwise_xor(device, 1 << s) * blocks),
            part,
        ]
        for s in range(strides)
    ]
    return jnp.concatenate([own[pl.ds(i * BLOCK, BLOCK), part]] + picked, 0)


def put_columns(ref, rows, head, columns, step=1, width=STAT_ROWS):
    held = ref[rows, :]
    lane = lax.broadcasted_iota(jnp.int32, held.shape, 1)
    for place, column in enumerate(columns):
        held = jnp.where(lane == head * width + place * step, column, held)
    ref[rows, :] = held


def take_column(ref, rows, head, place):
    held = ref[rows, :]
    lane = lax.broadcasted_iota(jnp.int32, held.shape, 1)
    return jnp.sum(jnp.where(lane == head * STAT_ROWS + place, held, 0.0), axis=1, keepdims=True)


NOTES = 7


def thirds(column):
    high = column.astype(BF16).astype(F32)
    middle = (column - high).astype(BF16).astype(F32)
    return high, middle, column - high - middle


def note_lines(rows, width):
    groups = width // rows
    lines = -(-NOTES * (width // HEAD_SIZE) // groups)
    return groups, -(-lines // 16) * 16


def read_notes(message, stats, rows, heads):
    _, lines = note_lines(rows, message.shape[1])
    held = message[message.shape[0] - lines :, :].astype(F32)

    def line(place, head):
        group, at = divmod(place * heads + head, lines)
        return held[at : at + 1, group * rows : (group + 1) * rows]

    for head in range(heads):
        for place, parts in enumerate(((0,), (1, 2, 3), (4, 5, 6))):
            at = head * STAT_ROWS + place
            stats[at : at + 1, :] = sum(line(part, head) for part in parts)


def near_kernel(strides, parts, cols_ref, query, grad, *refs):
    own_key, own_value = refs[:2]
    far_keys, far_values = refs[2 : 2 + strides], refs[2 + strides : 2 + 2 * strides]
    globs, owned = refs[2 + 2 * strides :][:parts], refs[2 + 2 * strides + parts : -6]
    weight_out, prob_out, glob_out, term_out, key_out, stats = refs[-6:]
    blocks, heads = query.shape[0] // BLOCK, query.shape[1] // HEAD_SIZE
    near, slots = (strides + 1) * BLOCK, key_out.shape[0]
    device = lax.axis_index("ctx")

    def one_head(head, _):
        part = columns_of(head)
        wide = pl.ds(pl.multiple_of(head * near, near), near)
        glob = pl.ds(pl.multiple_of(head * slots, slots), slots)
        glob_key = merged(globs, owned, part)
        key_out[:, part] = glob_key
        rounded = []
        for i in range(blocks):
            rows = pl.ds(i * BLOCK, BLOCK)
            keys = near_at(strides, device, blocks, i, cols_ref, own_key, far_keys, part)
            values = near_at(strides, device, blocks, i, cols_ref, own_value, far_values, part)
            scores = dot(query[rows, part], jnp.concatenate([keys, glob_key], 0), NT) * FACTOR
            prob_grad = dot(grad[rows, part], values, NT)
            top = jnp.max(scores, axis=1, keepdims=True)
            top = top.astype(BF16).astype(F32)
            exponent = jnp.exp(scores - top)
            scale = 1.0 / jnp.sum(exponent, axis=1, keepdims=True)
            weights = exponent * scale
            weight_out[rows, wide] = weights[:, :near]
            prob_out[rows, wide] = prob_grad
            glob_out[rows, glob] = weights[:, near:]
            rounded.append(weights[:, near:].astype(BF16))
            delta = jnp.sum(weights[:, :near] * prob_grad, axis=1, keepdims=True)
            put_columns(stats, rows, head, (top, scale, delta))
        term_out[:, part] = dot(jnp.concatenate(rounded, 0), grad[:, part], TN)

    lax.fori_loop(0, heads, one_head, None, unroll=2)


def glob_kernel(parts, query, grad, near_stats, weights_in, value_term, *refs):
    values_in, owned = refs[:parts], refs[parts : 2 * parts - 1]
    keep_on, keep_out, send_on, send_out, delta_out, score_out, value_out, stats = refs[2 * parts - 1 :]
    half, upper = keep_out.shape[0], bit_of(2)
    heads, slots = query.shape[1] // HEAD_SIZE, value_out.shape[0]
    odd = jnp.bitwise_and(lax.axis_index("ctx"), 1) == 1
    every = pl.ds(0, query.shape[0])

    def one_head(head, _):
        part = columns_of(head)
        glob = pl.ds(pl.multiple_of(head * slots, slots), slots)
        values = merged(values_in, owned, part)
        value_out[:, part] = values
        prob_grad = dot(grad[:, part], values, NT)
        top, scale, near_delta = (take_column(near_stats, every, head, place) for place in range(3))
        weights = weights_in[:, glob]
        delta = near_delta + jnp.sum(weights * prob_grad, axis=1, keepdims=True)
        score_grad = (weights * (prob_grad - delta)).astype(BF16)
        score_out[:, glob] = score_grad
        key_term = dot(score_grad, query[:, part], TN)
        keep = jnp.where(odd, value_term[:, part], key_term)
        send = jnp.where(odd, key_term, value_term[:, part])
        keep_on[:, part] = jnp.where(upper, keep[:half], keep[half:])
        keep_out[:, part] = jnp.where(upper, keep[half:], keep[:half])
        send_on[:, part] = jnp.where(upper, send[:half], send[half:]).astype(BF16)
        send_out[:half, part] = jnp.where(upper, send[half:], send[:half]).astype(BF16)
        notes = (top, *thirds(scale), *thirds(delta))
        put_columns(stats, every, head, notes, step=heads, width=1)
        put_columns(delta_out, every, head, (delta,))

    lax.fori_loop(0, heads, one_head, None, unroll=2)
    groups, lines = note_lines(query.shape[0], query.shape[1])
    for start in range(0, query.shape[0], BLOCK):
        turned = stats[pl.ds(start, BLOCK), :].T
        for group in range(groups):
            at = pl.ds(group * query.shape[0] + start, BLOCK)
            send_out[half:, at] = turned[group * lines : (group + 1) * lines].astype(BF16)


def rest_kernel(strides, cols_ref, weights_in, probs, deltas, glob_weights, scores_in, *refs):
    glob_key, glob_value, own_key, own_value = refs[:4]
    far_keys, far_values = refs[4 : 4 + strides], refs[4 + strides : 4 + 2 * strides]
    att_out, query_out = refs[-2:]
    blocks, heads = own_key.shape[0] // BLOCK, own_key.shape[1] // HEAD_SIZE
    near, slots = (strides + 1) * BLOCK, glob_key.shape[0]
    device = lax.axis_index("ctx")

    def one_head(head, _):
        part = columns_of(head)
        wide = pl.ds(pl.multiple_of(head * near, near), near)
        glob = pl.ds(pl.multiple_of(head * slots, slots), slots)
        for i in range(blocks):
            rows = pl.ds(i * BLOCK, BLOCK)
            keys = near_at(strides, device, blocks, i, cols_ref, own_key, far_keys, part)
            values = near_at(strides, device, blocks, i, cols_ref, own_value, far_values, part)
            delta = take_column(deltas, rows, head, 0)
            weights = weights_in[rows, wide]
            score_grad = (weights * (probs[rows, wide] - delta)).astype(BF16)
            attention = dot(weights.astype(BF16), values)
            attention = attention + dot(glob_weights[rows, glob].astype(BF16), glob_value[:, part])
            att_out[rows, part] = attention.astype(BF16)
            query_sum = dot(score_grad, keys) + dot(scores_in[rows, glob], glob_key[:, part])
            query_out[rows, part] = (query_sum * FACTOR).astype(BF16)

    lax.fori_loop(0, heads, one_head, None, unroll=2)


def key_kernel(s, count, cols_ref, key, value, *refs):
    *pair, message = refs[: count + 1]
    so_far, (key_out, value_out, stats) = refs[count + 1 : -3], refs[-3:]
    blocks = key.shape[0] // BLOCK
    heads = key.shape[1] // HEAD_SIZE
    device = lax.axis_index("ctx")
    read_notes(message, stats, key.shape[0], heads)
    grad_start = 0 if count > 1 else pair[0].shape[0] // 2

    def one_head(head, _):
        part = columns_of(head)
        stat_at = pl.multiple_of(head * STAT_ROWS, STAT_ROWS)
        if so_far:
            key_out[:, part] = so_far[0][:, part]
            value_out[:, part] = so_far[1][:, part]
        for i in range(blocks):
            rows = pl.ds(i * BLOCK, BLOCK)
            if s < 0:
                place = rows
            else:
                partner = jnp.bitwise_xor(device, 1 << s)
                place = block_at(cols_ref[s, partner * blocks + i] - device * blocks)
            q = pair[0][rows, part]
            g = pair[-1][pl.ds(grad_start + i * BLOCK, BLOCK), part]
            stat = stats[pl.ds(stat_at, STAT_ROWS), rows]
            top, scale, delta = stat[0:1], stat[1:2], stat[2:3]
            weights = jnp.exp(dot(key[place, part], q, NT) * FACTOR - top) * scale
            prob_grad = dot(value[place, part], g, NT)
            score_grad = (weights * (prob_grad - delta)).astype(BF16)
            key_term = dot(score_grad, q)
            value_term = dot(weights.astype(BF16), g)
            if s < 0:
                key_out[place, part] = key_term
                value_out[place, part] = value_term
            else:
                key_out[place, part] += key_term
                value_out[place, part] += value_term

    lax.fori_loop(0, heads, one_head, None)


def key_side(source, cols, key, value, pair, message, so_far=()):
    shape = like(key.shape, F32)
    heads = key.shape[1] // HEAD_SIZE
    return call(
        functools.partial(key_kernel, source, len(pair)),
        [shape, shape],
        cols,
        key,
        value,
        *pair,
        message,
        *so_far,
        scalars=1,
        scratch=[pltpu.VMEM((heads * STAT_ROWS, key.shape[0]), F32)],
    )


def bit_of(mask):
    return jnp.bitwise_and(lax.axis_index("ctx"), mask) != 0


def add_kernel(count, *refs):
    parts, mine, outs = refs[:count], refs[count], refs[count + 1 :]
    rows = parts[0].shape[0]
    result = sum((part[:rows, :].astype(F32) for part in parts[1:]), parts[0][...])
    for out in outs:
        out[:rows, :] = result.astype(out.dtype)
        if out.shape[0] > rows:
            out[rows:, :] = mine[rows:, :]


def add(parts, mine, *shapes):
    return call(functools.partial(add_kernel, len(parts)), list(shapes), *parts, mine)


def out_kernel(*refs):
    refs[-1][...] = sum((ref[...].astype(F32) for ref in refs[1:-1]), refs[0][...]).astype(BF16)


def final_kernel(cut, scatter, key, value, *refs):
    half = len(refs) // 2 - 1
    kept, got, (key_out, value_out) = refs[:half], refs[half:-2], refs[-2:]
    odd = bit_of(1)

    def rows_of(parts):
        if len(parts) == 1:
            return dot(scatter[...], parts[0][...])
        mine, other, upper = parts[0][...].astype(F32), parts[1][...].astype(F32), bit_of(cut)
        whole = [jnp.where(upper, other, mine), jnp.where(upper, mine, other)]
        return dot(scatter[...], jnp.concatenate(whole, 0).astype(BF16))

    kept_rows, got_rows = rows_of(kept), rows_of(got)
    key_rows = jnp.where(odd, got_rows, kept_rows)
    value_rows = jnp.where(odd, kept_rows, got_rows)
    key_out[...] = ((key[...] + key_rows) * FACTOR).astype(BF16)
    value_out[...] = (value[...] + value_rows).astype(BF16)


def finish(cut, scatter, key, value, kept, got):
    shape = jax.ShapeDtypeStruct(key.shape, BF16)
    kernel = functools.partial(final_kernel, cut)
    return call(kernel, [shape, shape], scatter, key, value, *kept, *got)


def per_device(query_act, key_act, value_act, out_weight, cotangent, butterfly_cols, global_cols):
    strides = butterfly_cols.shape[1]
    groups = lax.axis_size("head")
    cube = strides == 3 and lax.axis_size("ctx") == 1 << strides
    cols = butterfly_cols.T
    slots = global_cols.shape[0]
    rows, width = key_act.shape
    masks = [1 << s for s in range(strides)]
    held = (0, *masks) if cube else (0,)
    owners = ((3, 5), (6, 7)) if cube else ()

    own_key, own_value, scatter, *hot = call(
        functools.partial(hot_kernel, held, owners),
        [like((rows, width))] * 2
        + [like((rows, slots))]
        + [like((slots, rows))] * len(held)
        + [like((slots, HEAD_SIZE), F32)] * len(owners),
        global_cols.reshape(1, -1),
        outside=(key_act, value_act),
    )
    selects, owned = hot[: len(held)], hot[len(held) :]
    near_keys = [own_key] + [swap(key_act, "ctx", m) for m in masks]
    near_values = [own_value] + [swap(value_act, "ctx", m) for m in masks]
    pieces = [cotangent] + [swap(cotangent, "head", m) for m in range(1, groups)]
    if cube:
        glob = []
        for near in (near_keys, near_values):
            have = select_globals(selects, near)
            have = merge(have, swap(have, "ctx", 1), owned[0])
            glob.append([have, swap(have, "ctx", 2)])
        glob_keys, glob_values = glob
    else:
        parts = (select_globals(selects, [own_key]), select_globals(selects, [own_value]))
        glob_keys, glob_values = ([part] for part in lax.psum(parts, "ctx"))
    attn_grad, pair = call(
        grad_kernel, [like((rows, width)), like((2 * rows, width))], out_weight, query_act, *pieces
    )
    pairs = [[pair]] + [[swap(pair, "ctx", m)] for m in masks[:-1]]
    m = masks[-1]
    pairs.append([swap(query_act, "ctx", m), swap(attn_grad, "ctx", m)])
    near_all = [own_key, own_value, *near_keys[1:], *near_values[1:]]
    heads = width // HEAD_SIZE
    near = (strides + 1) * BLOCK
    weights, probs, glob_weights, value_term, glob_key, near_stats = call(
        functools.partial(near_kernel, strides, len(glob_keys)),
        [
            like((rows, heads * near), F32),
            like((rows, heads * near), F32),
            like((rows, heads * slots), F32),
            like((slots, width), F32),
            like((slots, width)),
            like((rows, BLOCK), F32),
        ],
        cols,
        query_act,
        attn_grad,
        *near_all,
        *glob_keys,
        *owned[1:],
        scalars=1,
    )
    notes = note_lines(rows, width)[1]
    keep_on, keep, send_on, message, deltas, scores, glob_value = call(
        functools.partial(glob_kernel, len(glob_values)),
        [
            like((slots // 2, width), F32),
            like((slots // 2, width), F32),
            like((slots // 2, width)),
            like((slots // 2 + notes, width)),
            like((rows, BLOCK), F32),
            like((rows, heads * slots)),
            like((slots, width)),
        ],
        query_act,
        attn_grad,
        near_stats,
        glob_weights,
        value_term,
        *glob_values,
        *owned[1:],
        scratch=[pltpu.VMEM((rows, BLOCK), F32)],
    )
    attention, query_grad = call(
        functools.partial(rest_kernel, strides),
        [like((rows, width)), jax.ShapeDtypeStruct((rows, width), BF16)],
        cols,
        weights,
        probs,
        deltas,
        glob_weights,
        scores,
        glob_key,
        glob_value,
        *near_all,
        scalars=1,
    )
    messages = [message]
    if cube:
        half = (slots // 2, width)
        came = swap(send_on, "ctx", 1)
        messages.append(swap(message, "ctx", 1))
        (message,) = add([keep_on, came], messages[0], like(messages[0].shape))
        messages.append(swap(message, "ctx", 2))
        total, message = add(
            [keep, *messages[1:]], messages[0], like(half, F32), like(messages[0].shape)
        )
        messages.append(swap(message, "ctx", 4))
        (mine,) = add([total, messages[3]], messages[0], like(half))
        other = swap(mine, "ctx", 2)
        kept = [mine, other]
        got = [swap(mine, "ctx", 1), swap(other, "ctx", 1)]
    else:
        messages += [swap(message, "ctx", m) for m in masks]
        odd, upper = (jnp.bitwise_and(lax.axis_index("ctx"), mask) != 0 for mask in (1, 2))
        sends = send_on.astype(F32), message[: slots // 2].astype(F32)
        halves = []
        for keep_half, send_half in zip((keep_on, keep), sends):
            halves.append(
                (jnp.where(odd, send_half, keep_half), jnp.where(odd, keep_half, send_half))
            )
        ordered = tuple(
            jnp.concatenate([jnp.where(upper, on, out), jnp.where(upper, out, on)], 0)
            for on, out in zip(*halves)
        )
        key_term, value_term = lax.psum(ordered, "ctx")
        kept = [jnp.where(odd, value_term, key_term).astype(BF16)]
        got = [jnp.where(odd, key_term, value_term).astype(BF16)]
    term = out_weight.shape[1] // groups
    shapes = [like((rows, term), F32 if m == 0 else BF16) for m in range(groups)]
    terms = call(project_kernel, shapes, attention, out_weight)
    parts = [swap(terms[m], "head", m) for m in range(1, groups)]
    out_shape = jax.ShapeDtypeStruct((rows, term), BF16)
    layer_out = call(out_kernel, [out_shape], terms[0], *parts)[0]
    so_far = ()
    for at, m in enumerate([0, *masks]):
        so_far = key_side(at - 1, cols, own_key, own_value, pairs[at], messages[at], so_far)
    key_sum, value_sum = so_far
    key_grad, value_grad = finish(2, scatter, key_sum, value_sum, kept, got)
    return (layer_out, query_grad, key_grad, value_grad)


def solution(mesh):
    in_specs = (
        P("ctx", "head"),
        P("ctx", "head"),
        P("ctx", "head"),
        P("head", None),
        P("ctx", "head"),
        P(),
        P(),
    )
    out_specs = (P("ctx", "head"),) * 4

    return jax.shard_map(
        per_device, mesh=mesh, in_specs=in_specs, out_specs=out_specs, check_vma=False
    )
```

```python
import functools
import math

import jax
import jax.numpy as jnp
from jax import lax
from jax.experimental import pallas as pl
from jax.experimental.pallas import tpu as pltpu
from jax.sharding import PartitionSpec as P


HEAD_SIZE = 128
BLOCK = 128
STAT_ROWS = 8
KERNEL_VMEM = 16 * 2**20


FACTOR = 1.0 / math.sqrt(HEAD_SIZE)
NT = (((1,), (1,)), ((), ()))
TN = (((0,), (0,)), ((), ()))
F32 = jnp.float32
BF16 = jnp.bfloat16


def swap(shard, axis, mask):
    return lax.ppermute(shard, axis, [(i, i ^ mask) for i in range(lax.axis_size(axis))])


def call(kernel, out_shape, *operands, scalars=0, scratch=(), outside=()):
    in_specs = [pl.BlockSpec(memory_space=pltpu.SMEM)] * scalars
    in_specs += [pl.BlockSpec(memory_space=pltpu.VMEM)] * (len(operands) - scalars + len(outside))
    outs = [pl.BlockSpec(memory_space=pltpu.VMEM)] * len(out_shape)
    placed = [pltpu.with_memory_space_constraint(o, pltpu.VMEM) for o in operands[scalars:]]
    return pl.pallas_call(
        kernel,
        in_specs=in_specs,
        out_specs=outs,
        out_shape=out_shape,
        scratch_shapes=scratch,
        compiler_params=pltpu.CompilerParams(vmem_limit_bytes=KERNEL_VMEM),
    )(*operands[:scalars], *placed, *outside)


def like(shape, dtype=jnp.bfloat16):
    return pltpu.VMEM(shape, dtype)


def dot(a, b, dims=(((1,), (0,)), ((), ()))):
    return lax.dot_general(a, b, dims, preferred_element_type=F32)


def block_at(index):
    return pl.ds(pl.multiple_of(index * BLOCK, BLOCK), BLOCK)


def columns_of(head):
    return pl.ds(pl.multiple_of(head * HEAD_SIZE, HEAD_SIZE), HEAD_SIZE)


def grad_kernel(weight_ref, query, *refs):
    pieces, (out_ref, pair_ref) = refs[:-2], refs[-2:]
    rows = query.shape[0]
    width = pieces[0].shape[1]
    mine = lax.axis_index("head")
    total = None
    for m, piece in enumerate(pieces):
        start = pl.multiple_of(jnp.bitwise_xor(mine, m) * width, width)
        part = dot(piece[...], weight_ref[:, pl.ds(start, width)], NT)
        total = part if total is None else total + part
    out_ref[...] = total.astype(BF16)
    pair_ref[:rows, :] = query[...]
    pair_ref[rows:, :] = total.astype(BF16)


def project_kernel(att_ref, weight_ref, *outs):
    width = outs[0].shape[1]
    mine = lax.axis_index("head")
    for m, out in enumerate(outs):
        start = pl.multiple_of(jnp.bitwise_xor(mine, m) * width, width)
        out[...] = dot(att_ref[...], weight_ref[:, pl.ds(start, width)]).astype(out.dtype)


def hot_kernel(masks, groups, cols_ref, key, value, key_copy, value_copy, scatter_ref, *outs):
    key_copy[...] = key[...]
    value_copy[...] = value[...]
    rows, slots = scatter_ref.shape
    device = lax.axis_index("ctx")
    row_ids = lax.broadcasted_iota(jnp.int32, (rows, slots), 0)

    def local(mask):
        return cols_ref[...] - jnp.bitwise_xor(device, mask) * rows

    for mask, out in zip(masks, outs):
        chosen = (row_ids == local(mask)).astype(F32)
        if mask == 0:
            scatter_ref[...] = chosen.astype(BF16)
        out[...] = chosen.T.astype(BF16)
    for group, out in zip(groups, outs[len(masks) :]):
        owned = 0.0
        for mask in group:
            at = jnp.broadcast_to(local(mask), (out.shape[1], slots))
            owned = owned + jnp.logical_and(at >= 0, at < rows).astype(F32)
        out[...] = owned.T


def select_kernel(count, *refs):
    total = dot(refs[0][...], refs[count][...])
    for select, source in zip(refs[1:count], refs[count + 1 : -1]):
        total = total + dot(select[...], source[...])
    refs[-1][...] = total.astype(BF16)


def select_globals(selects, sources):
    shape = like((selects[0].shape[0], sources[0].shape[1]))
    kernel = functools.partial(select_kernel, len(selects))
    return call(kernel, [shape], *selects, *sources)[0]


def merged(parts, owned, at):
    total = parts[0][:, at].astype(F32)
    for part, mask in zip(parts[1:], owned):
        total = total + mask[...] * part[:, at].astype(F32)
    return total.astype(BF16)


def merge_kernel(have, got, owned, out):
    for start in range(0, out.shape[1], HEAD_SIZE):
        part = pl.ds(start, HEAD_SIZE)
        out[:, part] = merged((have, got), (owned,), part)


def merge(have, got, owned):
    return call(merge_kernel, [like(have.shape)], have, got, owned)[0]


def near_at(strides, device, blocks, i, cols_ref, own, far, part):
    picked = [
        far[s][
            block_at(cols_ref[s, device * blocks + i] - jnp.bitwise_xor(device, 1 << s) * blocks),
            part,
        ]
        for s in range(strides)
    ]
    return jnp.concatenate([own[pl.ds(i * BLOCK, BLOCK), part]] + picked, 0)


def put_columns(ref, rows, head, columns, step=1, width=STAT_ROWS):
    held = ref[rows, :]
    lane = lax.broadcasted_iota(jnp.int32, held.shape, 1)
    for place, column in enumerate(columns):
        held = jnp.where(lane == head * width + place * step, column, held)
    ref[rows, :] = held


def take_column(ref, rows, head, place):
    held = ref[rows, :]
    lane = lax.broadcasted_iota(jnp.int32, held.shape, 1)
    return jnp.sum(jnp.where(lane == head * STAT_ROWS + place, held, 0.0), axis=1, keepdims=True)


NOTES = 7


def thirds(column):
    high = column.astype(BF16).astype(F32)
    middle = (column - high).astype(BF16).astype(F32)
    return high, middle, column - high - middle


def note_lines(rows, width):
    groups = width // rows
    lines = -(-NOTES * (width // HEAD_SIZE) // groups)
    return groups, -(-lines // 16) * 16


def read_notes(message, stats, rows, heads):
    _, lines = note_lines(rows, message.shape[1])
    held = message[message.shape[0] - lines :, :].astype(F32)

    def line(place, head):
        group, at = divmod(place * heads + head, lines)
        return held[at : at + 1, group * rows : (group + 1) * rows]

    for head in range(heads):
        for place, parts in enumerate(((0,), (1, 2, 3), (4, 5, 6))):
            at = head * STAT_ROWS + place
            stats[at : at + 1, :] = sum(line(part, head) for part in parts)


def near_kernel(strides, parts, cols_ref, query, grad, *refs):
    own_key, own_value = refs[:2]
    far_keys, far_values = refs[2 : 2 + strides], refs[2 + strides : 2 + 2 * strides]
    globs, owned = refs[2 + 2 * strides :][:parts], refs[2 + 2 * strides + parts : -6]
    weight_out, prob_out, glob_out, term_out, key_out, stats = refs[-6:]
    blocks, heads = query.shape[0] // BLOCK, query.shape[1] // HEAD_SIZE
    near, slots = (strides + 1) * BLOCK, key_out.shape[0]
    device = lax.axis_index("ctx")

    def one_head(head, _):
        part = columns_of(head)
        wide = pl.ds(pl.multiple_of(head * near, near), near)
        glob = pl.ds(pl.multiple_of(head * slots, slots), slots)
        glob_key = merged(globs, owned, part)
        key_out[:, part] = glob_key
        rounded = []
        for i in range(blocks):
            rows = pl.ds(i * BLOCK, BLOCK)
            keys = near_at(strides, device, blocks, i, cols_ref, own_key, far_keys, part)
            values = near_at(strides, device, blocks, i, cols_ref, own_value, far_values, part)
            scores = dot(query[rows, part], jnp.concatenate([keys, glob_key], 0), NT) * FACTOR
            prob_grad = dot(grad[rows, part], values, NT)
            top = jnp.max(scores, axis=1, keepdims=True)
            top = top.astype(BF16).astype(F32)
            exponent = jnp.exp(scores - top)
            scale = 1.0 / jnp.sum(exponent, axis=1, keepdims=True)
            weights = exponent * scale
            weight_out[rows, wide] = weights[:, :near]
            prob_out[rows, wide] = prob_grad
            glob_out[rows, glob] = weights[:, near:]
            rounded.append(weights[:, near:].astype(BF16))
            delta = jnp.sum(weights[:, :near] * prob_grad, axis=1, keepdims=True)
            put_columns(stats, rows, head, (top, scale, delta))
        term_out[:, part] = dot(jnp.concatenate(rounded, 0), grad[:, part], TN)

    lax.fori_loop(0, heads, one_head, None, unroll=4)


def glob_kernel(parts, query, grad, near_stats, weights_in, value_term, *refs):
    values_in, owned = refs[:parts], refs[parts : 2 * parts - 1]
    keep_on, keep_out, send_on, send_out, delta_out, score_out, value_out, stats = refs[2 * parts - 1 :]
    half, upper = keep_out.shape[0], bit_of(2)
    heads, slots = query.shape[1] // HEAD_SIZE, value_out.shape[0]
    odd = jnp.bitwise_and(lax.axis_index("ctx"), 1) == 1
    every = pl.ds(0, query.shape[0])

    def one_head(head, _):
        part = columns_of(head)
        glob = pl.ds(pl.multiple_of(head * slots, slots), slots)
        values = merged(values_in, owned, part)
        value_out[:, part] = values
        prob_grad = dot(grad[:, part], values, NT)
        top, scale, near_delta = (take_column(near_stats, every, head, place) for place in range(3))
        weights = weights_in[:, glob]
        delta = near_delta + jnp.sum(weights * prob_grad, axis=1, keepdims=True)
        score_grad = (weights * (prob_grad - delta)).astype(BF16)
        score_out[:, glob] = score_grad
        key_term = dot(score_grad, query[:, part], TN)
        keep = jnp.where(odd, value_term[:, part], key_term)
        send = jnp.where(odd, key_term, value_term[:, part])
        keep_on[:, part] = jnp.where(upper, keep[:half], keep[half:])
        keep_out[:, part] = jnp.where(upper, keep[half:], keep[:half])
        send_on[:, part] = jnp.where(upper, send[:half], send[half:]).astype(BF16)
        send_out[:half, part] = jnp.where(upper, send[half:], send[:half]).astype(BF16)
        notes = (top, *thirds(scale), *thirds(delta))
        put_columns(stats, every, head, notes, step=heads, width=1)
        put_columns(delta_out, every, head, (delta,))

    lax.fori_loop(0, heads, one_head, None, unroll=4)
    groups, lines = note_lines(query.shape[0], query.shape[1])
    for start in range(0, query.shape[0], BLOCK):
        turned = stats[pl.ds(start, BLOCK), :].T
        for group in range(groups):
            at = pl.ds(group * query.shape[0] + start, BLOCK)
            send_out[half:, at] = turned[group * lines : (group + 1) * lines].astype(BF16)


def rest_kernel(strides, cols_ref, weights_in, probs, deltas, glob_weights, scores_in, *refs):
    glob_key, glob_value, own_key, own_value = refs[:4]
    far_keys, far_values = refs[4 : 4 + strides], refs[4 + strides : 4 + 2 * strides]
    att_out, query_out = refs[-2:]
    blocks, heads = own_key.shape[0] // BLOCK, own_key.shape[1] // HEAD_SIZE
    near, slots = (strides + 1) * BLOCK, glob_key.shape[0]
    device = lax.axis_index("ctx")

    def one_head(head, _):
        part = columns_of(head)
        wide = pl.ds(pl.multiple_of(head * near, near), near)
        glob = pl.ds(pl.multiple_of(head * slots, slots), slots)
        for i in range(blocks):
            rows = pl.ds(i * BLOCK, BLOCK)
            keys = near_at(strides, device, blocks, i, cols_ref, own_key, far_keys, part)
            values = near_at(strides, device, blocks, i, cols_ref, own_value, far_values, part)
            delta = take_column(deltas, rows, head, 0)
            weights = weights_in[rows, wide]
            score_grad = (weights * (probs[rows, wide] - delta)).astype(BF16)
            attention = dot(weights.astype(BF16), values)
            attention = attention + dot(glob_weights[rows, glob].astype(BF16), glob_value[:, part])
            att_out[rows, part] = attention.astype(BF16)
            query_sum = dot(score_grad, keys) + dot(scores_in[rows, glob], glob_key[:, part])
            query_out[rows, part] = (query_sum * FACTOR).astype(BF16)

    lax.fori_loop(0, heads, one_head, None, unroll=4)


def key_kernel(s, count, cols_ref, key, value, *refs):
    *pair, message = refs[: count + 1]
    so_far, (key_out, value_out, stats) = refs[count + 1 : -3], refs[-3:]
    blocks = key.shape[0] // BLOCK
    heads = key.shape[1] // HEAD_SIZE
    device = lax.axis_index("ctx")
    read_notes(message, stats, key.shape[0], heads)
    grad_start = 0 if count > 1 else pair[0].shape[0] // 2

    def one_head(head, _):
        part = columns_of(head)
        stat_at = pl.multiple_of(head * STAT_ROWS, STAT_ROWS)
        if so_far:
            key_out[:, part] = so_far[0][:, part]
            value_out[:, part] = so_far[1][:, part]
        for i in range(blocks):
            rows = pl.ds(i * BLOCK, BLOCK)
            if s < 0:
                place = rows
            else:
                partner = jnp.bitwise_xor(device, 1 << s)
                place = block_at(cols_ref[s, partner * blocks + i] - device * blocks)
            q = pair[0][rows, part]
            g = pair[-1][pl.ds(grad_start + i * BLOCK, BLOCK), part]
            stat = stats[pl.ds(stat_at, STAT_ROWS), rows]
            top, scale, delta = stat[0:1], stat[1:2], stat[2:3]
            weights = jnp.exp(dot(key[place, part], q, NT) * FACTOR - top) * scale
            prob_grad = dot(value[place, part], g, NT)
            score_grad = (weights * (prob_grad - delta)).astype(BF16)
            key_term = dot(score_grad, q)
            value_term = dot(weights.astype(BF16), g)
            if s < 0:
                key_out[place, part] = key_term
                value_out[place, part] = value_term
            else:
                key_out[place, part] += key_term
                value_out[place, part] += value_term

    lax.fori_loop(0, heads, one_head, None, unroll=4)


def key_side(source, cols, key, value, pair, message, so_far=()):
    shape = like(key.shape, F32)
    heads = key.shape[1] // HEAD_SIZE
    return call(
        functools.partial(key_kernel, source, len(pair)),
        [shape, shape],
        cols,
        key,
        value,
        *pair,
        message,
        *so_far,
        scalars=1,
        scratch=[pltpu.VMEM((heads * STAT_ROWS, key.shape[0]), F32)],
    )


def bit_of(mask):
    return jnp.bitwise_and(lax.axis_index("ctx"), mask) != 0


def add_kernel(count, *refs):
    parts, mine, outs = refs[:count], refs[count], refs[count + 1 :]
    rows = parts[0].shape[0]
    result = sum((part[:rows, :].astype(F32) for part in parts[1:]), parts[0][...])
    for out in outs:
        out[:rows, :] = result.astype(out.dtype)
        if out.shape[0] > rows:
            out[rows:, :] = mine[rows:, :]


def add(parts, mine, *shapes):
    return call(functools.partial(add_kernel, len(parts)), list(shapes), *parts, mine)


def out_kernel(*refs):
    refs[-1][...] = sum((ref[...].astype(F32) for ref in refs[1:-1]), refs[0][...]).astype(BF16)


def final_kernel(cut, scatter, key, value, *refs):
    half = len(refs) // 2 - 1
    kept, got, (key_out, value_out) = refs[:half], refs[half:-2], refs[-2:]
    odd = bit_of(1)

    def rows_of(parts):
        if len(parts) == 1:
            return dot(scatter[...], parts[0][...])
        mine, other, upper = parts[0][...].astype(F32), parts[1][...].astype(F32), bit_of(cut)
        whole = [jnp.where(upper, other, mine), jnp.where(upper, mine, other)]
        return dot(scatter[...], jnp.concatenate(whole, 0).astype(BF16))

    kept_rows, got_rows = rows_of(kept), rows_of(got)
    key_rows = jnp.where(odd, got_rows, kept_rows)
    value_rows = jnp.where(odd, kept_rows, got_rows)
    key_out[...] = ((key[...] + key_rows) * FACTOR).astype(BF16)
    value_out[...] = (value[...] + value_rows).astype(BF16)


def finish(cut, scatter, key, value, kept, got):
    shape = jax.ShapeDtypeStruct(key.shape, BF16)
    kernel = functools.partial(final_kernel, cut)
    return call(kernel, [shape, shape], scatter, key, value, *kept, *got)


def per_device(query_act, key_act, value_act, out_weight, cotangent, butterfly_cols, global_cols):
    strides = butterfly_cols.shape[1]
    groups = lax.axis_size("head")
    cube = strides == 3 and lax.axis_size("ctx") == 1 << strides
    cols = butterfly_cols.T
    slots = global_cols.shape[0]
    rows, width = key_act.shape
    masks = [1 << s for s in range(strides)]
    held = (0, *masks) if cube else (0,)
    owners = ((3, 5), (6, 7)) if cube else ()

    own_key, own_value, scatter, *hot = call(
        functools.partial(hot_kernel, held, owners),
        [like((rows, width))] * 2
        + [like((rows, slots))]
        + [like((slots, rows))] * len(held)
        + [like((slots, HEAD_SIZE), F32)] * len(owners),
        global_cols.reshape(1, -1),
        outside=(key_act, value_act),
    )
    selects, owned = hot[: len(held)], hot[len(held) :]
    near_keys = [own_key] + [swap(key_act, "ctx", m) for m in masks]
    near_values = [own_value] + [swap(value_act, "ctx", m) for m in masks]
    pieces = [cotangent] + [swap(cotangent, "head", m) for m in range(1, groups)]
    if cube:
        glob = []
        for near in (near_keys, near_values):
            have = select_globals(selects, near)
            have = merge(have, swap(have, "ctx", 1), owned[0])
            glob.append([have, swap(have, "ctx", 2)])
        glob_keys, glob_values = glob
    else:
        parts = (select_globals(selects, [own_key]), select_globals(selects, [own_value]))
        glob_keys, glob_values = ([part] for part in lax.psum(parts, "ctx"))
    attn_grad, pair = call(
        grad_kernel, [like((rows, width)), like((2 * rows, width))], out_weight, query_act, *pieces
    )
    pairs = [[pair]] + [[swap(pair, "ctx", m)] for m in masks[:-1]]
    m = masks[-1]
    pairs.append([swap(query_act, "ctx", m), swap(attn_grad, "ctx", m)])
    near_all = [own_key, own_value, *near_keys[1:], *near_values[1:]]
    heads = width // HEAD_SIZE
    near = (strides + 1) * BLOCK
    weights, probs, glob_weights, value_term, glob_key, near_stats = call(
        functools.partial(near_kernel, strides, len(glob_keys)),
        [
            like((rows, heads * near), F32),
            like((rows, heads * near), F32),
            like((rows, heads * slots), F32),
            like((slots, width), F32),
            like((slots, width)),
            like((rows, BLOCK), F32),
        ],
        cols,
        query_act,
        attn_grad,
        *near_all,
        *glob_keys,
        *owned[1:],
        scalars=1,
    )
    notes = note_lines(rows, width)[1]
    keep_on, keep, send_on, message, deltas, scores, glob_value = call(
        functools.partial(glob_kernel, len(glob_values)),
        [
            like((slots // 2, width), F32),
            like((slots // 2, width), F32),
            like((slots // 2, width)),
            like((slots // 2 + notes, width)),
            like((rows, BLOCK), F32),
            like((rows, heads * slots)),
            like((slots, width)),
        ],
        query_act,
        attn_grad,
        near_stats,
        glob_weights,
        value_term,
        *glob_values,
        *owned[1:],
        scratch=[pltpu.VMEM((rows, BLOCK), F32)],
    )
    attention, query_grad = call(
        functools.partial(rest_kernel, strides),
        [like((rows, width)), jax.ShapeDtypeStruct((rows, width), BF16)],
        cols,
        weights,
        probs,
        deltas,
        glob_weights,
        scores,
        glob_key,
        glob_value,
        *near_all,
        scalars=1,
    )
    messages = [message]
    if cube:
        half = (slots // 2, width)
        came = swap(send_on, "ctx", 1)
        messages.append(swap(message, "ctx", 1))
        (message,) = add([keep_on, came], messages[0], like(messages[0].shape))
        messages.append(swap(message, "ctx", 2))
        total, message = add(
            [keep, *messages[1:]], messages[0], like(half, F32), like(messages[0].shape)
        )
        messages.append(swap(message, "ctx", 4))
        (mine,) = add([total, messages[3]], messages[0], like(half))
        other = swap(mine, "ctx", 2)
        kept = [mine, other]
        got = [swap(mine, "ctx", 1), swap(other, "ctx", 1)]
    else:
        messages += [swap(message, "ctx", m) for m in masks]
        odd, upper = (jnp.bitwise_and(lax.axis_index("ctx"), mask) != 0 for mask in (1, 2))
        sends = send_on.astype(F32), message[: slots // 2].astype(F32)
        halves = []
        for keep_half, send_half in zip((keep_on, keep), sends):
            halves.append(
                (jnp.where(odd, send_half, keep_half), jnp.where(odd, keep_half, send_half))
            )
        ordered = tuple(
            jnp.concatenate([jnp.where(upper, on, out), jnp.where(upper, out, on)], 0)
            for on, out in zip(*halves)
        )
        key_term, value_term = lax.psum(ordered, "ctx")
        kept = [jnp.where(odd, value_term, key_term).astype(BF16)]
        got = [jnp.where(odd, key_term, value_term).astype(BF16)]
    term = out_weight.shape[1] // groups
    shapes = [like((rows, term), F32 if m == 0 else BF16) for m in range(groups)]
    terms = call(project_kernel, shapes, attention, out_weight)
    parts = [swap(terms[m], "head", m) for m in range(1, groups)]
    out_shape = jax.ShapeDtypeStruct((rows, term), BF16)
    layer_out = call(out_kernel, [out_shape], terms[0], *parts)[0]
    so_far = ()
    for at, m in enumerate([0, *masks]):
        so_far = key_side(at - 1, cols, own_key, own_value, pairs[at], messages[at], so_far)
    key_sum, value_sum = so_far
    key_grad, value_grad = finish(2, scatter, key_sum, value_sum, kept, got)
    return (layer_out, query_grad, key_grad, value_grad)


def solution(mesh):
    in_specs = (
        P("ctx", "head"),
        P("ctx", "head"),
        P("ctx", "head"),
        P("head", None),
        P("ctx", "head"),
        P(),
        P(),
    )
    out_specs = (P("ctx", "head"),) * 4

    return jax.shard_map(
        per_device, mesh=mesh, in_specs=in_specs, out_specs=out_specs, check_vma=False
    )
```
